256 devices in a mesh: rows: 64 (over z_hi, x, y), rank: 4 (over z_lo, core).
Axes of the slice: x: 4, y: 4, z: 8 (z_hi: 4, z_lo: 2; z = z_hi * 2 + z_lo), core: 2. Of those that a mesh axis runs over, the one named last changes fastest.
Arguments:
- control: bfloat16 [1024, 64, 8, 128], P('rank', 'rows'), may hold values from -6 to 6
- observe: bfloat16 [1024, 8, 128, 64], P('rank', None, 'rows'), may hold values from -6 to 6
- capacity: float32 [64, 8, 128], P('rows'), may hold values from 0.5 to 2
- conduct: float32 [64, 8, 128], P('rows'), may hold values from 0.5 to 2
Outputs:
- left_basis: bfloat16 [1024, 64, 8, 128], P('rank', 'rows')
- stiff_basis: bfloat16 [1024, 64, 8, 128], P('rank', 'rows')
The draws below stay inside these ranges and needn't reach their ends.
All inputs are finite; a program needn't handle non-finite values.
Results may differ from the reference program's by a relative error of at most 0.0067.
Values may be sent and summed in bfloat16 or wider, within the bound.
No kernel may reach another device: no remote copies, remote signals or barrier semaphores. Data moves between devices by JAX's collectives and lax.ppermute only.
A program may use at most 128 MiB of HBM per device.

```python
import math
import jax
import jax.numpy as jnp
from jax import lax

R = 1024
NZ = 8
NY = 128
NX = 64


def block_scale(key, shape, split, least, top_value):
    factor_of = 1.0
    for axis_at, shards_of in split:
        steps = jax.random.uniform(jax.random.fold_in(jax.random.fold_in(key, 6), axis_at), (shards_of,), jnp.float32, least / len(split), top_value / len(split))
        factor_of = factor_of * jnp.repeat(jnp.exp(steps), shape[axis_at] // shards_of).reshape((-1,) + (1,) * (len(shape) - 1 - axis_at))
    return factor_of


def gaussian(key, shape, scale, most, cuts=(), kind=jnp.bfloat16):
    factor_of = block_scale(key, shape, cuts, -0.22, 0.18) if cuts else 1.0
    array = jax.random.normal(key, shape, jnp.float32) * scale * factor_of
    return jnp.minimum(jnp.maximum(array, -most), most).astype(kind)


def setup_inputs(seed: int = 0) -> dict:
    seeds = jax.random.split(jax.random.key(seed), 5)
    return {
        "control": gaussian(seeds[0], (R, NX, NZ, NY), 1.0, 6.0, ((0, 4), (1, 64))),
        "observe": gaussian(seeds[1], (R, NZ, NY, NX), 1.0, 6.0, ((0, 4), (2, 64))),
        "capacity": jnp.clip(jnp.exp(math.log(2.0) - 1.3862944 * jax.random.uniform(seeds[2], (NX, NZ, NY), jnp.float32) ** block_scale(seeds[2], (NX, NZ, NY), ((0, 64),), -0.2, 0.2)), 0.5, 2.0),
        "conduct": jnp.clip(jnp.exp(math.log(2.0) - 1.3862944 * jax.random.uniform(seeds[3], (NX, NZ, NY), jnp.float32) ** block_scale(seeds[3], (NX, NZ, NY), ((0, 64),), -0.2, 0.2)), 0.5, 2.0),
    }


ONE_SIXTH = 1.0 / 6.0

def spread(padded, along_dim, side_weight, centre):
    length = padded.shape[along_dim] - 2
    before = lax.slice_in_dim(padded, 0, length, axis=along_dim)
    middle = lax.slice_in_dim(padded, 1, length + 1, axis=along_dim)
    beyond = lax.slice_in_dim(padded, 2, length + 2, axis=along_dim)
    return side_weight * (before + beyond) + centre * middle

def apply_line(values, along_dim, side_weight, centre):
    widths = [(0, 0)] * values.ndim
    widths[along_dim] = (1, 1)
    return spread(jnp.pad(values, widths), along_dim, side_weight, centre)

def mass_apply(padded):
    result = spread(padded, 1, ONE_SIXTH, 4.0 * ONE_SIXTH)
    result = apply_line(result, 2, ONE_SIXTH, 4.0 * ONE_SIXTH)
    return apply_line(result, 3, ONE_SIXTH, 4.0 * ONE_SIXTH)

def stiff_apply(padded):
    mass_x = spread(padded, 1, ONE_SIXTH, 4.0 * ONE_SIXTH)
    stiff_x = spread(padded, 1, -1.0, 2.0)
    first = apply_line(apply_line(stiff_x, 3, ONE_SIXTH, 4.0 * ONE_SIXTH), 2, ONE_SIXTH, 4.0 * ONE_SIXTH)
    second = apply_line(apply_line(mass_x, 3, -1.0, 2.0), 2, ONE_SIXTH, 4.0 * ONE_SIXTH)
    third = apply_line(apply_line(mass_x, 3, ONE_SIXTH, 4.0 * ONE_SIXTH), 2, -1.0, 2.0)
    return first + second + third

def reference(control, observe, capacity, conduct):
    col_block = math.gcd(R, 128)
    shaped = control.reshape(R // col_block, col_block, NX, NZ, NY)

    def mass_part(factor_block):
        scaled = (capacity * factor_block.astype(jnp.float32)).astype(jnp.bfloat16)
        widened = jnp.pad(scaled, ((0, 0), (1, 1), (0, 0), (0, 0)))
        return (capacity * mass_apply(widened.astype(jnp.float32))).astype(jnp.bfloat16)
    applied = lax.map(mass_part, shaped).reshape(R, NX * NZ * NY)
    relaid = jnp.transpose(observe, (0, 3, 1, 2)).reshape(R, NX * NZ * NY)
    control_flat = control.reshape(R, NX * NZ * NY)
    crossed = lax.dot_general(relaid.astype(jnp.float32), applied.astype(jnp.float32), (((1,), (1,)), ((), ())), preferred_element_type=jnp.float32)
    level = jnp.sum(crossed * crossed) / R + 1e-06
    normed = crossed / jnp.sqrt(level)
    identity = jnp.eye(R, dtype=jnp.float32)
    gram = jnp.dot(normed.T.astype(jnp.float32), normed.astype(jnp.float32), precision=lax.Precision.HIGHEST, preferred_element_type=jnp.float32) + identity
    chol = jnp.linalg.cholesky(gram)
    solved = lax.linalg.triangular_solve(chol, jnp.concatenate([identity, normed.T], axis=1), left_side=True, lower=True)
    inverse_low = solved[:, :R].astype(jnp.bfloat16)
    project_low = solved[:, R:].astype(jnp.bfloat16)
    right_basis = jnp.dot(inverse_low.astype(jnp.float32), control_flat.astype(jnp.float32), preferred_element_type=jnp.float32)
    left_basis = jnp.dot(project_low.astype(jnp.float32), relaid.astype(jnp.float32), preferred_element_type=jnp.float32).astype(jnp.bfloat16)
    left_basis = left_basis.reshape(R, NX, NZ, NY)

    def stiff_part(basis_block):
        scaled = (conduct * basis_block).astype(jnp.bfloat16)
        widened = jnp.pad(scaled, ((0, 0), (1, 1), (0, 0), (0, 0)))
        return (-(conduct * stiff_apply(widened.astype(jnp.float32)))).astype(jnp.bfloat16)
    stiff_basis = lax.map(stiff_part, right_basis.reshape(R // col_block, col_block, NX, NZ, NY))
    return (left_basis, stiff_basis.reshape(R, NX, NZ, NY))
```

```python
import jax
import jax.numpy as jnp
from jax import lax
from jax.experimental import pallas as pl
from jax.experimental.pallas import tpu as pltpu
from jax.sharding import Mesh
from jax.sharding import PartitionSpec as P

ONE_SIXTH = 1.0 / 6.0
F32 = jnp.float32
BF16 = jnp.bfloat16
ROWS = ("zh", "x", "y")
RANK = ("zl", "core")
COLS = 1024
OWN = 256
SIDE = 128
TILES = COLS // SIDE
LANES = 128


def extended(x, axis, dim):
    devices, length = (lax.axis_size(axis), x.shape[dim])
    up = [(i, (i + 1) % devices) for i in range(devices - 1)]
    down = [(j, i) for i, j in up]
    before = lax.ppermute(lax.slice_in_dim(x, length - 1, length, axis=dim), axis, up)
    after = lax.ppermute(lax.slice_in_dim(x, 0, 1, axis=dim), axis, down)
    return jnp.concatenate([before, x, after], axis=dim)


def spread(padded, along_dim, side_weight, centre):
    length = padded.shape[along_dim] - 2
    before = lax.slice_in_dim(padded, 0, length, axis=along_dim)
    middle = lax.slice_in_dim(padded, 1, length + 1, axis=along_dim)
    beyond = lax.slice_in_dim(padded, 2, length + 2, axis=along_dim)
    return side_weight * (before + beyond) + centre * middle


def apply_line(values, along_dim, side_weight, centre):
    widths = [(0, 0)] * values.ndim
    widths[along_dim] = (1, 1)
    return spread(jnp.pad(values, widths), along_dim, side_weight, centre)


def mass_apply(padded):
    result = spread(padded, 1, ONE_SIXTH, 4.0 * ONE_SIXTH)
    result = apply_line(result, 2, ONE_SIXTH, 4.0 * ONE_SIXTH)
    return apply_line(result, 3, ONE_SIXTH, 4.0 * ONE_SIXTH)


def stiff_apply(padded):
    mass_x = spread(padded, 1, ONE_SIXTH, 4.0 * ONE_SIXTH)
    stiff_x = spread(padded, 1, -1.0, 2.0)
    first = apply_line(
        apply_line(stiff_x, 3, ONE_SIXTH, 4.0 * ONE_SIXTH), 2, ONE_SIXTH, 4.0 * ONE_SIXTH
    )
    second = apply_line(apply_line(mass_x, 3, -1.0, 2.0), 2, ONE_SIXTH, 4.0 * ONE_SIXTH)
    third = apply_line(apply_line(mass_x, 3, ONE_SIXTH, 4.0 * ONE_SIXTH), 2, -1.0, 2.0)
    return first + second + third


def halves(x):
    high = x.astype(BF16)
    return high, (x - high.astype(F32)).astype(BF16)


def product(a, b, a_dim=1, b_dim=0):
    dims = (((a_dim,), (b_dim,)), ((), ()))

    def one(p, q):
        return lax.dot_general(p, q, dims, preferred_element_type=F32)

    return one(a[0], b[0]) + (one(a[0], b[1]) + one(a[1], b[0]))


def factor_block(block):
    lane = lax.broadcasted_iota(jnp.int32, (8, SIDE), 1)
    sub = lax.broadcasted_iota(jnp.int32, (8, SIDE), 0)
    rows = [block[8 * v : 8 * v + 8, :] for v in range(SIDE // 8)]
    for j in range(SIDE):
        first, s = divmod(j, 8)
        row = jnp.broadcast_to(rows[first][s : s + 1, :], (8, SIDE))
        inverse = 1.0 / jnp.broadcast_to(row[:, j : j + 1], (8, SIDE))
        here = lane == j
        pivot_row = jnp.where(here, inverse, row * inverse)
        for v in range(first, SIDE // 8):
            if v == first and s == 7:
                continue
            column = jnp.broadcast_to(rows[v][:, j : j + 1], (8, SIDE))
            updated = jnp.where(here, 0.0, rows[v]) - column * pivot_row
            rows[v] = jnp.where(sub > s, updated, rows[v]) if v == first else updated
    out = []
    for v in range(SIDE // 8):
        on_diagonal = lane == sub + 8 * v
        pivots = jnp.sum(jnp.where(on_diagonal, rows[v], 0.0), axis=1, keepdims=True)
        scale = lax.rsqrt(pivots)
        scale = scale * (1.5 - 0.5 * pivots * scale * scale)
        low = jnp.where(lane < sub + 8 * v, rows[v], jnp.where(on_diagonal, 1.0, 0.0))
        out.append(low * scale)
    return jnp.concatenate(out, axis=0)


def factor_kernel(where, left, right, left_other, right_other, inv_out, proj_out, high, low, m):
    core = where[1]
    total = jnp.zeros((1, 1), F32)
    for half, pair in enumerate(((left, left_other), (right, right_other))):
        for chip in range(2):
            for other, source in enumerate(pair):
                block = chip * 2 + (core if other == 0 else 1 - core)
                lanes = pl.ds(pl.multiple_of(block * OWN + half * LANES, LANES), LANES)
                x = source[chip]
                total = total + jnp.sum(
                    jnp.sum(x * x, axis=0, keepdims=True), axis=1, keepdims=True
                )
                upper, lower = halves(x)
                high[:, lanes] = upper
                low[:, lanes] = lower
    level = total / COLS + 1e-6
    scale = 1.0 / level
    eye = (
        lax.broadcasted_iota(jnp.int32, (SIDE, SIDE), 0)
        == lax.broadcasted_iota(jnp.int32, (SIDE, SIDE), 1)
    ).astype(F32)
    for k in range(TILES):
        block = slice(k * SIDE, (k + 1) * SIDE)
        a = (high[block, :], low[block, :])
        m[block, k * SIDE :] = product(a, (high[k * SIDE :, :], low[k * SIDE :, :]), 1, 1) * scale
        m[block, block] = m[block, block] + eye
    for k in range(TILES):
        block = slice(k * SIDE, (k + 1) * SIDE)
        x = factor_block(m[block, block])
        x_halves = halves(x)
        if k:
            m[block, : k * SIDE] = product(x_halves, halves(m[block, : k * SIDE]))
        m[block, block] = x
        if k + 1 < TILES:
            r = product(x_halves, halves(m[block, (k + 1) * SIDE :]))
            r_halves = halves(r)
            done = halves(m[block, : (k + 1) * SIDE])
            for i in range(k + 1, TILES):
                rows = slice(i * SIDE, (i + 1) * SIDE)
                at = (i - k - 1) * SIDE
                mine = tuple(part[:, at : at + SIDE] for part in r_halves)
                rest = tuple(part[:, at:] for part in r_halves)
                m[rows, i * SIDE :] = m[rows, i * SIDE :] - product(mine, rest, 0, 0)
                taken = product(mine, done, 0, 0)
                if k:
                    m[rows, : k * SIDE] = m[rows, : k * SIDE] - taken[:, : k * SIDE]
                m[rows, block] = -taken[:, k * SIDE :]
            m[block, (k + 1) * SIDE :] = jnp.zeros_like(r)
    own = m[pl.ds(pl.multiple_of(where[0] * OWN, OWN), OWN), :]
    inv_out[...] = own.astype(BF16)
    proj_out[...] = (product(halves(own), (high[...], low[...])) * lax.rsqrt(level)).astype(BF16)


def factor(where, left, right, left_other, right_other):
    vmem = pl.BlockSpec(memory_space=pltpu.VMEM)
    return pl.pallas_call(
        factor_kernel,
        out_shape=(jax.ShapeDtypeStruct((OWN, COLS), BF16),) * 2,
        in_specs=[pl.BlockSpec(memory_space=pltpu.SMEM)] + [vmem] * 4,
        out_specs=[vmem] * 2,
        scratch_shapes=[
            pltpu.VMEM((COLS, COLS), BF16),
            pltpu.VMEM((COLS, COLS), BF16),
            pltpu.VMEM((COLS, COLS), F32),
        ],
        compiler_params=pltpu.CompilerParams(vmem_limit_bytes=48 * 2**20),
    )(where, left, right, left_other, right_other)

def gather_four(x, axis, dim):
    here = lax.axis_index(axis)
    shape = list(x.shape)
    shape[dim] = 4
    full = lax.dynamic_update_slice_in_dim(jnp.zeros(shape, x.dtype), x, here, dim)
    for step in (1, 2, 3):
        moved = lax.ppermute(x, axis, [(d, (d + step) % 4) for d in range(4)])
        full = lax.dynamic_update_slice_in_dim(full, moved, (here - step) % 4, dim)
    return full


def body(control, observe, capacity, conduct):
    col_rows = control.shape[0]
    local_cells = control.shape[1] * control.shape[2] * control.shape[3]
    scaled = (capacity * control.astype(F32)).astype(BF16)
    widened = extended(scaled, ROWS, 1)
    applied = (capacity * mass_apply(widened.astype(F32))).astype(BF16)
    applied_flat = applied.reshape(col_rows, local_cells)
    relaid = jnp.transpose(
        lax.all_to_all(observe, ROWS, split_axis=3, concat_axis=2, tiled=True), (0, 3, 1, 2)
    )
    relaid_flat = relaid.reshape(col_rows, local_cells)
    control_flat = control.reshape(col_rows, local_cells)
    part = lax.dot_general(
        lax.all_gather(applied_flat, RANK, axis=0, tiled=True),
        relaid_flat,
        (((1,), (1,)), ((), ())),
        preferred_element_type=F32,
    )
    pieces = lax.all_to_all(part, ROWS, split_axis=0, concat_axis=0, tiled=True)
    summed = jnp.sum(pieces.reshape(64, COLS // 64, OWN), axis=0)
    low = lax.axis_index("zl") == 0
    other = lax.ppermute(summed, "zl", [(0, 1), (1, 0)])
    pair = jnp.stack([jnp.where(low, summed, other), jnp.where(low, other, summed)])
    pair = gather_four(pair.reshape(2, 1, 1, 1, COLS // 64, OWN), "zh", 1)
    left_half = gather_four(pair[..., :LANES], "x", 2)
    right_half = gather_four(pair[..., LANES:], "y", 3)
    left_half = gather_four(left_half, "y", 3).reshape(2, COLS, LANES)
    right_half = gather_four(right_half, "x", 2).reshape(2, COLS, LANES)
    swap = [(0, 1), (1, 0)]
    left_other = lax.ppermute(left_half, "core", swap)
    right_other = lax.ppermute(right_half, "core", swap)
    where = jnp.stack([lax.axis_index(RANK), lax.axis_index("core")]).astype(jnp.int32)
    inverse_low, project_low = factor(where, left_half, right_half, left_other, right_other)
    right_basis = jnp.dot(
        inverse_low,
        lax.all_gather(control_flat, RANK, axis=0, tiled=True),
        preferred_element_type=F32,
    )
    left_sum = jnp.dot(
        project_low,
        lax.all_gather(relaid_flat, RANK, axis=0, tiled=True),
        preferred_element_type=F32,
    )
    left_basis = left_sum.astype(BF16).reshape(control.shape)
    scaled_right = (conduct * right_basis.reshape(control.shape)).astype(BF16)
    widened_right = extended(scaled_right, ROWS, 1)
    stiff_basis = (-(conduct * stiff_apply(widened_right.astype(F32)))).astype(BF16)
    return (left_basis, stiff_basis)


def solution(mesh):
    torus = Mesh(mesh.devices.reshape(4, 4, 4, 2, 2), ROWS + RANK)
    in_specs = (
        P(RANK, ROWS, None, None),
        P(RANK, None, ROWS, None),
        P(ROWS, None, None),
        P(ROWS, None, None),
    )
    out_specs = (P(RANK, ROWS, None, None), P(RANK, ROWS, None, None))
    return jax.shard_map(body, mesh=torus, in_specs=in_specs, out_specs=out_specs, check_vma=False)
```

```python
import jax
import jax.numpy as jnp
from jax import lax
from jax.experimental import pallas as pl
from jax.experimental.pallas import tpu as pltpu
from jax.sharding import Mesh
from jax.sharding import PartitionSpec as P


ONE_SIXTH = 1.0 / 6.0
F32 = jnp.float32
BF16 = jnp.bfloat16
ROWS = ("zh", "x", "y")
RANK = ("zl", "core")
COLS = 1024
OWN = 256
SIDE = 128
TILES = COLS // SIDE
LANES = 128
GROUP = 8


def extended(x, axis, dim):
    devices, length = (lax.axis_size(axis), x.shape[dim])
    up = [(i, (i + 1) % devices) for i in range(devices - 1)]
    down = [(j, i) for i, j in up]
    before = lax.ppermute(lax.slice_in_dim(x, length - 1, length, axis=dim), axis, up)
    after = lax.ppermute(lax.slice_in_dim(x, 0, 1, axis=dim), axis, down)
    return jnp.concatenate([before, x, after], axis=dim)


def spread(padded, along_dim, side_weight, centre):
    length = padded.shape[along_dim] - 2
    before = lax.slice_in_dim(padded, 0, length, axis=along_dim)
    middle = lax.slice_in_dim(padded, 1, length + 1, axis=along_dim)
    beyond = lax.slice_in_dim(padded, 2, length + 2, axis=along_dim)
    return side_weight * (before + beyond) + centre * middle


def apply_line(values, along_dim, side_weight, centre):
    widths = [(0, 0)] * values.ndim
    widths[along_dim] = (1, 1)
    return spread(jnp.pad(values, widths), along_dim, side_weight, centre)


def mass_apply(padded):
    result = spread(padded, 1, ONE_SIXTH, 4.0 * ONE_SIXTH)
    result = apply_line(result, 2, ONE_SIXTH, 4.0 * ONE_SIXTH)
    return apply_line(result, 3, ONE_SIXTH, 4.0 * ONE_SIXTH)


def stiff_apply(padded):
    mass_x = spread(padded, 1, ONE_SIXTH, 4.0 * ONE_SIXTH)
    stiff_x = spread(padded, 1, -1.0, 2.0)
    first = apply_line(
        apply_line(stiff_x, 3, ONE_SIXTH, 4.0 * ONE_SIXTH), 2, ONE_SIXTH, 4.0 * ONE_SIXTH
    )
    second = apply_line(apply_line(mass_x, 3, -1.0, 2.0), 2, ONE_SIXTH, 4.0 * ONE_SIXTH)
    third = apply_line(apply_line(mass_x, 3, ONE_SIXTH, 4.0 * ONE_SIXTH), 2, -1.0, 2.0)
    return first + second + third


def halves(x):
    high = x.astype(BF16)
    return high, (x - high.astype(F32)).astype(BF16)

def product(a, b, a_dim=1, b_dim=0):
    dims = (((a_dim,), (b_dim,)), ((), ()))
    def one(p, q):
        return lax.dot_general(p, q, dims, preferred_element_type=F32)
    return one(a[0], b[0]) + (one(a[0], b[1]) + one(a[1], b[0]))

def factor_block(block):
    lane = lax.broadcasted_iota(jnp.int32, (GROUP, SIDE), 1)
    sub = lax.broadcasted_iota(jnp.int32, (GROUP, SIDE), 0)
    wide = lambda row: jnp.broadcast_to(row, (GROUP, SIDE))
    count = SIDE // GROUP
    rows = [block[GROUP * v : GROUP * (v + 1), :] for v in range(count)]
    out = []
    for g in range(count):
        base = g * GROUP
        inside = (lane >= base) & (lane < base + GROUP)
        own = [wide(rows[g][:, base + t : base + t + 1]) for t in range(GROUP)]
        body = jnp.where(inside, 0.0, rows[g])
        pivots = jnp.ones((GROUP, SIDE), F32)
        uppers, inverses, pivot_rows = [], [], []
        for s in range(GROUP):
            pivot = wide(own[s][s : s + 1, :])
            inverse = 1.0 / pivot
            upper = {t: wide(own[t][s : s + 1, :]) for t in range(s + 1, GROUP)}
            taken = jnp.where(sub > s, own[s] * inverse, 0.0)
            pivot_row = jnp.where(lane == base + s, 1.0, wide(body[s : s + 1, :]))
            for t in range(s + 1, GROUP):
                own[t] = own[t] - taken * upper[t]
            body = body - taken * pivot_row
            pivots = jnp.where(sub == s, pivot, pivots)
            uppers.append(upper); inverses.append(inverse); pivot_rows.append(pivot_row)
        for v in range(g + 1, count):
            cols = [wide(rows[v][:, base + t : base + t + 1]) for t in range(GROUP)]
            new = jnp.where(inside, 0.0, rows[v])
            for s in range(GROUP):
                taken = cols[s] * inverses[s]
                for t in range(s + 1, GROUP):
                    cols[t] = cols[t] - taken * uppers[s][t]
                new = new - taken * pivot_rows[s]
            rows[v] = new
        low = jnp.where(lane == sub + base, 1.0, jnp.where(lane < base + GROUP, body, 0.0))
        scale = lax.rsqrt(pivots)
        scale = scale * (1.5 - 0.5 * pivots * scale * scale)
        out.append(low * scale)
    return jnp.concatenate(out, axis=0)

def factor_kernel(where, left, right, left_other, right_other, inv_out, proj_out, high, low, m, r_high, r_low):
    core = where[1]
    total = jnp.zeros((1, 1), F32)
    for half, pair in enumerate(((left, left_other), (right, right_other))):
        for chip in range(2):
            for other, source in enumerate(pair):
                block = chip * 2 + (core if other == 0 else 1 - core)
                lanes = pl.ds(pl.multiple_of(block * OWN + half * LANES, LANES), LANES)
                for turn in range(4):
                    x = source[chip, turn * OWN : (turn + 1) * OWN, :]
                    total = total + jnp.sum(
                        jnp.sum(x * x, axis=0, keepdims=True), axis=1, keepdims=True
                    )
                    upper, lower = halves(x)
                    rows = pl.ds(pl.multiple_of(((block + turn) % 4) * OWN, OWN), OWN)
                    high[rows, lanes] = upper
                    low[rows, lanes] = lower
    level = total / COLS + 1e-6
    scale = 1.0 / level
    eye = (lax.broadcasted_iota(jnp.int32, (SIDE, SIDE), 0) == lax.broadcasted_iota(jnp.int32, (SIDE, SIDE), 1)).astype(F32)
    for k in range(TILES):
        block = slice(k * SIDE, (k + 1) * SIDE)
        a = (high[block, :], low[block, :])
        m[block, k * SIDE :] = product(a, (high[k * SIDE :, :], low[k * SIDE :, :]), 1, 1) * scale
        m[block, block] = m[block, block] + eye
        if k:
            m[block, : k * SIDE] = jnp.zeros((SIDE, k * SIDE), F32)

    def step(k, carry):
        block = pl.ds(pl.multiple_of(k * SIDE, SIDE), SIDE)
        x = factor_block(m[block, block])
        m[block, block] = eye
        r = product(halves(x), halves(m[block, :]))
        m[block, :] = r
        upper, lower = halves(r)
        r_high[...] = upper
        r_low[...] = lower

        def update(i, inner):
            rows = pl.ds(pl.multiple_of(i * SIDE, SIDE), SIDE)
            m[rows, block] = jnp.zeros((SIDE, SIDE), F32)
            mine = (r_high[:, rows], r_low[:, rows])
            m[rows, :] = m[rows, :] - product(mine, (r_high[...], r_low[...]), 0, 0)
            return inner

        lax.fori_loop(k + 1, TILES, update, 0)
        return carry

    lax.fori_loop(0, TILES, step, 0)
    first = pl.multiple_of(where[0] * OWN, OWN)
    row = lax.broadcasted_iota(jnp.int32, (OWN, OWN), 0)
    column = lax.broadcasted_iota(jnp.int32, (OWN, OWN), 1)
    own = []
    for block in range(4):
        part = m[pl.ds(first, OWN), block * OWN : (block + 1) * OWN]
        own.append(jnp.where(column + block * OWN <= row + first, part, 0.0))
    own = halves(jnp.concatenate(own, axis=1))
    shrink = lax.rsqrt(level)
    for turn in range(4):
        block = (where[0] + turn) % 4
        lanes = pl.ds(pl.multiple_of(block * OWN, OWN), OWN)
        out = slice(turn * OWN, (turn + 1) * OWN)
        part = m[pl.ds(first, OWN), lanes]
        part = jnp.where(column + block * OWN <= row + first, part, 0.0)
        inv_out[:, out] = part.astype(BF16)
        proj_out[:, out] = (product(own, (high[:, lanes], low[:, lanes])) * shrink).astype(BF16)


def factor(where, left, right, left_other, right_other):
    vmem = pl.BlockSpec(memory_space=pltpu.VMEM)
    return pl.pallas_call(
        factor_kernel,
        out_shape=(jax.ShapeDtypeStruct((OWN, COLS), BF16),) * 2,
        in_specs=[pl.BlockSpec(memory_space=pltpu.SMEM)] + [vmem] * 4,
        out_specs=[vmem] * 2,
        scratch_shapes=[
            pltpu.VMEM((COLS, COLS), BF16),
            pltpu.VMEM((COLS, COLS), BF16),
            pltpu.VMEM((COLS, COLS), F32),
            pltpu.VMEM((SIDE, COLS), BF16),
            pltpu.VMEM((SIDE, COLS), BF16),
        ],
        compiler_params=pltpu.CompilerParams(vmem_limit_bytes=20 * 2**20),
    )(where, left, right, left_other, right_other)


def gather_four(x, axis, dim):
    here = lax.axis_index(axis)
    shape = list(x.shape)
    shape[dim] = 4
    full = lax.dynamic_update_slice_in_dim(jnp.zeros(shape, x.dtype), x, here, dim)
    for step in (1, 2, 3):
        moved = lax.ppermute(x, axis, [(d, (d + step) % 4) for d in range(4)])
        full = lax.dynamic_update_slice_in_dim(full, moved, (here - step) % 4, dim)
    return full


def turned(x):
    moved = [lax.ppermute(x, RANK, [(d, (d - step) % 4) for d in range(4)]) for step in (1, 2, 3)]
    return jnp.concatenate([x] + moved, axis=0)


def body(control, observe, capacity, conduct):
    col_rows = control.shape[0]
    local_cells = control.shape[1] * control.shape[2] * control.shape[3]
    scaled = (capacity * control.astype(F32)).astype(BF16)
    widened = extended(scaled, ROWS, 1)
    applied = (capacity * mass_apply(widened.astype(F32))).astype(BF16)
    applied_all = turned(applied.reshape(col_rows, local_cells))
    relaid = jnp.transpose(
        lax.all_to_all(observe, ROWS, split_axis=3, concat_axis=2, tiled=True), (0, 3, 1, 2)
    )
    relaid_flat = relaid.reshape(col_rows, local_cells)
    control_flat = control.reshape(col_rows, local_cells)
    part = lax.dot_general(
        applied_all, relaid_flat, (((1,), (1,)), ((), ())), preferred_element_type=F32
    )
    pieces = lax.all_to_all(part, ("x", "y"), split_axis=0, concat_axis=0, tiled=True)
    chunk = jnp.sum(pieces.reshape(16, COLS // 16, OWN), axis=0)
    summed = chunk
    for step in (1, 2, 3):
        summed = summed + lax.ppermute(chunk, "zh", [(d, (d + step) % 4) for d in range(4)])
    swap = [(0, 1), (1, 0)]
    low = lax.axis_index("zl") == 0
    other = lax.ppermute(summed, "zl", swap)
    pair = jnp.stack([jnp.where(low, summed, other), jnp.where(low, other, summed)])
    pair = pair.reshape(2, 1, 1, COLS // 16, OWN)
    left_half = gather_four(pair[..., :LANES], "x", 1)
    right_half = gather_four(pair[..., LANES:], "y", 2)
    left_half = gather_four(left_half, "y", 2).reshape(2, COLS, LANES)
    right_half = gather_four(right_half, "x", 1).reshape(2, COLS, LANES)
    left_other = lax.ppermute(left_half, "core", swap)
    right_other = lax.ppermute(right_half, "core", swap)
    control_flat, relaid_flat, left_other, right_other = lax.optimization_barrier(
        (control_flat, relaid_flat, left_other, right_other)
    )
    control_all = turned(control_flat)
    relaid_all = turned(relaid_flat)
    where = jnp.stack([lax.axis_index(RANK), lax.axis_index("core")]).astype(jnp.int32)
    inverse_low, project_low = factor(where, left_half, right_half, left_other, right_other)
    right_basis = jnp.dot(inverse_low, control_all, preferred_element_type=F32)
    scaled_right = (conduct * right_basis.reshape(control.shape)).astype(BF16)
    widened_right = extended(scaled_right, ROWS, 1)
    left_sum = jnp.dot(project_low, relaid_all, preferred_element_type=F32)
    left_basis = left_sum.astype(BF16).reshape(control.shape)
    stiff_basis = (-(conduct * stiff_apply(widened_right.astype(F32)))).astype(BF16)
    return (left_basis, stiff_basis)


def solution(mesh):
    torus = Mesh(mesh.devices.reshape(4, 4, 4, 2, 2), ROWS + RANK)
    in_specs = (
        P(RANK, ROWS, None, None),
        P(RANK, None, ROWS, None),
        P(ROWS, None, None),
        P(ROWS, None, None),
    )
    out_specs = (P(RANK, ROWS, None, None), P(RANK, ROWS, None, None))
    return jax.shard_map(body, mesh=torus, in_specs=in_specs, out_specs=out_specs, check_vma=False)
```

```python
import jax
import jax.numpy as jnp
from jax import lax
from jax.experimental import pallas as pl
from jax.experimental.pallas import tpu as pltpu
from jax.sharding import Mesh
from jax.sharding import PartitionSpec as P


ONE_SIXTH = 1.0 / 6.0
F32 = jnp.float32
BF16 = jnp.bfloat16
ROWS = ("zh", "x", "y")
RANK = ("zl", "core")
COLS = 1024
OWN = 256
SIDE = 128
TILES = COLS // SIDE
LANES = 128
GROUP = 8


def extended(x, axis, dim):
    devices, length = (lax.axis_size(axis), x.shape[dim])
    up = [(i, (i + 1) % devices) for i in range(devices - 1)]
    down = [(j, i) for i, j in up]
    before = lax.ppermute(lax.slice_in_dim(x, length - 1, length, axis=dim), axis, up)
    after = lax.ppermute(lax.slice_in_dim(x, 0, 1, axis=dim), axis, down)
    return jnp.concatenate([before, x, after], axis=dim)


def spread(padded, along_dim, side_weight, centre):
    length = padded.shape[along_dim] - 2
    before = lax.slice_in_dim(padded, 0, length, axis=along_dim)
    middle = lax.slice_in_dim(padded, 1, length + 1, axis=along_dim)
    beyond = lax.slice_in_dim(padded, 2, length + 2, axis=along_dim)
    return side_weight * (before + beyond) + centre * middle


def apply_line(values, along_dim, side_weight, centre):
    widths = [(0, 0)] * values.ndim
    widths[along_dim] = (1, 1)
    return spread(jnp.pad(values, widths), along_dim, side_weight, centre)


def mass_apply(padded):
    result = spread(padded, 1, ONE_SIXTH, 4.0 * ONE_SIXTH)
    result = apply_line(result, 2, ONE_SIXTH, 4.0 * ONE_SIXTH)
    return apply_line(result, 3, ONE_SIXTH, 4.0 * ONE_SIXTH)


def stiff_apply(padded):
    mass_x = spread(padded, 1, ONE_SIXTH, 4.0 * ONE_SIXTH)
    stiff_x = spread(padded, 1, -1.0, 2.0)
    first = apply_line(
        apply_line(stiff_x, 3, ONE_SIXTH, 4.0 * ONE_SIXTH), 2, ONE_SIXTH, 4.0 * ONE_SIXTH
    )
    second = apply_line(apply_line(mass_x, 3, -1.0, 2.0), 2, ONE_SIXTH, 4.0 * ONE_SIXTH)
    third = apply_line(apply_line(mass_x, 3, ONE_SIXTH, 4.0 * ONE_SIXTH), 2, -1.0, 2.0)
    return first + second + third


def halves(x):
    high = x.astype(BF16)
    return high, (x - high.astype(F32)).astype(BF16)

def product(a, b, a_dim=1, b_dim=0):
    dims = (((a_dim,), (b_dim,)), ((), ()))
    def one(p, q):
        return lax.dot_general(p, q, dims, preferred_element_type=F32)
    return one(a[0], b[0]) + (one(a[0], b[1]) + one(a[1], b[0]))

def factor_block(block):
    lane = lax.broadcasted_iota(jnp.int32, (GROUP, SIDE), 1)
    sub = lax.broadcasted_iota(jnp.int32, (GROUP, SIDE), 0)
    count = SIDE // GROUP

    def wide(row):
        return jnp.broadcast_to(row, (GROUP, SIDE))

    def columns(tile, base):
        return [wide(tile[:, base + t : base + t + 1]) for t in range(GROUP)]

    rows = [block[GROUP * v : GROUP * (v + 1), :] for v in range(count)]
    own = columns(rows[0], 0)
    out = []
    for g in range(count):
        base = g * GROUP
        inside = (lane >= base) & (lane < base + GROUP)
        body = jnp.where(inside, 0.0, rows[g])
        pivots = jnp.ones((GROUP, SIDE), F32)
        uppers, inverses, pivot_rows = [], [], []
        for s in range(GROUP):
            pivot = wide(own[s][s : s + 1, :])
            inverse = 1.0 / pivot
            upper = {t: wide(own[t][s : s + 1, :]) for t in range(s + 1, GROUP)}
            taken = jnp.where(sub > s, own[s] * inverse, 0.0)
            pivot_row = jnp.where(lane == base + s, 1.0, wide(body[s : s + 1, :]))
            for t in range(s + 1, GROUP):
                own[t] = own[t] - taken * upper[t]
            body = body - taken * pivot_row
            pivots = jnp.where(sub == s, pivot, pivots)
            uppers.append(upper)
            inverses.append(inverse)
            pivot_rows.append(pivot_row)
        for v in range(g + 1, count):
            cols = columns(rows[v], base)
            new = jnp.where(inside, 0.0, rows[v])
            ahead = columns(rows[v], base + GROUP) if v == g + 1 else []
            for s in range(GROUP):
                taken = cols[s] * inverses[s]
                ahead = [a - taken * wide(cols[s][t : t + 1, :]) for t, a in enumerate(ahead)]
                for t in range(s + 1, GROUP):
                    cols[t] = cols[t] - taken * uppers[s][t]
                new = new - taken * pivot_rows[s]
            rows[v] = new
            own = ahead or own
        low = jnp.where(lane == sub + base, 1.0, jnp.where(lane < base + GROUP, body, 0.0))
        scale = lax.rsqrt(pivots)
        scale = scale * (1.5 - 0.5 * pivots * scale * scale)
        out.append(low * scale)
    return jnp.concatenate(out, axis=0)


def factor_kernel(where, left, right, left_other, right_other, inv_out, proj_out, high, low, m, r_high, r_low):
    core = where[1]
    strip = OWN // 4

    def load(r, squares):
        inner = pl.ds(pl.multiple_of(r * strip, strip), strip)
        for half, pair in enumerate(((left, left_other), (right, right_other))):
            for chip in range(2):
                for other, source in enumerate(pair):
                    block = chip * 2 + (core if other == 0 else 1 - core)
                    lanes = pl.ds(pl.multiple_of(block * OWN + half * LANES, LANES), LANES)
                    x = source[chip, inner, :]
                    for at in range(0, strip, GROUP):
                        squares = squares + x[at : at + GROUP] * x[at : at + GROUP]
                    upper, lower = halves(x)
                    target = (block ^ (r // 4)) * OWN + (r % 4) * strip
                    rows = pl.ds(pl.multiple_of(target, strip), strip)
                    high[rows, lanes] = upper
                    low[rows, lanes] = lower
        return squares

    squares = lax.fori_loop(0, COLS // strip, load, jnp.zeros((GROUP, LANES), F32))
    total = jnp.sum(jnp.sum(squares, axis=0, keepdims=True), axis=1, keepdims=True)
    level = total / COLS + 1e-6
    scale = 1.0 / level
    eye = (lax.broadcasted_iota(jnp.int32, (SIDE, SIDE), 0) == lax.broadcasted_iota(jnp.int32, (SIDE, SIDE), 1)).astype(F32)
    def gram(a, carry):
        left_rows = pl.ds(pl.multiple_of(a * OWN, OWN), OWN)

        def one(b, inner):
            right_rows = pl.ds(pl.multiple_of(b * OWN, OWN), OWN)
            pair = product(
                (high[left_rows, :], low[left_rows, :]),
                (high[right_rows, :], low[right_rows, :]),
                1,
                1,
            )
            m[left_rows, right_rows] = pair * scale
            return inner

        return lax.fori_loop(a, COLS // OWN, one, carry)

    lax.fori_loop(0, COLS // OWN, gram, 0)

    def step(k, carry):
        block = pl.ds(pl.multiple_of(k * SIDE, SIDE), SIDE)
        x = factor_block(m[block, block] + eye)
        m[block, block] = eye
        r = product(halves(x), halves(m[block, :]))
        m[block, :] = r
        upper, lower = halves(r)
        r_high[...] = upper
        r_low[...] = lower

        def update(i, inner):
            rows = pl.ds(pl.multiple_of(i * SIDE, SIDE), SIDE)
            m[rows, block] = jnp.zeros((SIDE, SIDE), F32)
            mine = (r_high[:, rows], r_low[:, rows])
            m[rows, :] = m[rows, :] - product(mine, (r_high[...], r_low[...]), 0, 0)
            return inner

        lax.fori_loop(k + 1, TILES, update, 0)
        return carry

    lax.fori_loop(0, TILES, step, 0)
    first = pl.multiple_of(where[0] * OWN, OWN)
    row = lax.broadcasted_iota(jnp.int32, (OWN, OWN), 0)
    column = lax.broadcasted_iota(jnp.int32, (OWN, OWN), 1)
    own = []
    for block in range(4):
        part = m[pl.ds(first, OWN), block * OWN : (block + 1) * OWN]
        own.append(jnp.where(column + block * OWN <= row + first, part, 0.0))
    own = halves(jnp.concatenate(own, axis=1))
    shrink = lax.rsqrt(level)
    def project(turn, carry):
        block = where[0] ^ turn
        lanes = pl.ds(pl.multiple_of(block * OWN, OWN), OWN)
        out = pl.ds(pl.multiple_of(turn * OWN, OWN), OWN)
        part = m[pl.ds(first, OWN), lanes]
        part = jnp.where(column + block * OWN <= row + first, part, 0.0)
        inv_out[:, out] = part.astype(BF16)
        proj_out[:, out] = (product(own, (high[:, lanes], low[:, lanes])) * shrink).astype(BF16)
        return carry

    lax.fori_loop(0, 4, project, 0)


def factor(where, left, right, left_other, right_other):
    vmem = pl.BlockSpec(memory_space=pltpu.VMEM)
    return pl.pallas_call(
        factor_kernel,
        out_shape=(jax.ShapeDtypeStruct((OWN, COLS), BF16),) * 2,
        in_specs=[pl.BlockSpec(memory_space=pltpu.SMEM)] + [vmem] * 4,
        out_specs=[vmem] * 2,
        scratch_shapes=[
            pltpu.VMEM((COLS, COLS), BF16),
            pltpu.VMEM((COLS, COLS), BF16),
            pltpu.VMEM((COLS, COLS), F32),
            pltpu.VMEM((SIDE, COLS), BF16),
            pltpu.VMEM((SIDE, COLS), BF16),
        ],
        compiler_params=pltpu.CompilerParams(vmem_limit_bytes=20 * 2**20),
    )(where, left, right, left_other, right_other)


def gather_four(x, axis, dim):
    here = lax.axis_index(axis)
    shape = list(x.shape)
    shape[dim] = 4
    full = lax.dynamic_update_slice_in_dim(jnp.zeros(shape, x.dtype), x, here, dim)
    for step in (1, 2, 3):
        moved = lax.ppermute(x, axis, [(d, (d + step) % 4) for d in range(4)])
        full = lax.dynamic_update_slice_in_dim(full, moved, (here - step) % 4, dim)
    return full


def turned(x):
    moved = [lax.ppermute(x, RANK, [(d, d ^ step) for d in range(4)]) for step in (1, 2, 3)]
    return jnp.concatenate([x] + moved, axis=0)


def relayed(x):
    swap = [(0, 1), (1, 0)]
    near = lax.ppermute(x, "core", swap)
    across = lax.ppermute(x, "zl", swap)
    return jnp.concatenate([x, near, across, lax.ppermute(across, "core", swap)], axis=0)


def body(control, observe, capacity, conduct):
    col_rows = control.shape[0]
    local_cells = control.shape[1] * control.shape[2] * control.shape[3]
    scaled = (capacity * control.astype(F32)).astype(BF16)
    widened = extended(scaled, ROWS, 1)
    applied = (capacity * mass_apply(widened.astype(F32))).astype(BF16)
    applied_all = relayed(applied.reshape(col_rows, local_cells))
    relaid = jnp.transpose(
        lax.all_to_all(observe, ROWS, split_axis=3, concat_axis=2, tiled=True), (0, 3, 1, 2)
    )
    relaid_flat = relaid.reshape(col_rows, local_cells)
    control_flat = control.reshape(col_rows, local_cells)
    part = lax.dot_general(
        applied_all, relaid_flat, (((1,), (1,)), ((), ())), preferred_element_type=F32
    )
    pieces = lax.all_to_all(part, ("x", "y"), split_axis=0, concat_axis=0, tiled=True)
    chunk = jnp.sum(pieces.reshape(16, COLS // 16, OWN), axis=0)
    summed = chunk
    for step in (1, 2, 3):
        summed = summed + lax.ppermute(chunk, "zh", [(d, (d + step) % 4) for d in range(4)])
    swap = [(0, 1), (1, 0)]
    low = lax.axis_index("zl") == 0
    other = lax.ppermute(summed, "zl", swap)
    pair = jnp.stack([jnp.where(low, summed, other), jnp.where(low, other, summed)])
    pair = pair.reshape(2, 1, 1, COLS // 16, OWN)
    left_half = gather_four(pair[..., :LANES], "x", 1)
    right_half = gather_four(pair[..., LANES:], "y", 2)
    left_half = gather_four(left_half, "y", 2).reshape(2, COLS, LANES)
    right_half = gather_four(right_half, "x", 1).reshape(2, COLS, LANES)
    left_other = lax.ppermute(left_half, "core", swap)
    right_other = lax.ppermute(right_half, "core", swap)
    control_flat, relaid_flat, left_other, right_other = lax.optimization_barrier(
        (control_flat, relaid_flat, left_other, right_other)
    )
    control_all = turned(control_flat)
    relaid_all = turned(relaid_flat)
    where = jnp.stack([lax.axis_index(RANK), lax.axis_index("core")]).astype(jnp.int32)
    inverse_low, project_low = factor(where, left_half, right_half, left_other, right_other)
    right_basis = jnp.dot(inverse_low, control_all, preferred_element_type=F32)
    scaled_right = (conduct * right_basis.reshape(control.shape)).astype(BF16)
    widened_right = extended(scaled_right, ROWS, 1)
    left_sum = jnp.dot(project_low, relaid_all, preferred_element_type=F32)
    left_basis = left_sum.astype(BF16).reshape(control.shape)
    stiff_basis = (-(conduct * stiff_apply(widened_right.astype(F32)))).astype(BF16)
    return (left_basis, stiff_basis)


def solution(mesh):
    torus = Mesh(mesh.devices.reshape(4, 4, 4, 2, 2), ROWS + RANK)
    in_specs = (
        P(RANK, ROWS, None, None),
        P(RANK, None, ROWS, None),
        P(ROWS, None, None),
        P(ROWS, None, None),
    )
    out_specs = (P(RANK, ROWS, None, None), P(RANK, ROWS, None, None))
    return jax.shard_map(body, mesh=torus, in_specs=in_specs, out_specs=out_specs, check_vma=False)
```

```python
import jax
import jax.numpy as jnp
from jax import lax
from jax.experimental import pallas as pl
from jax.experimental.pallas import tpu as pltpu
from jax.sharding import Mesh
from jax.sharding import PartitionSpec as P


ONE_SIXTH = 1.0 / 6.0
F32 = jnp.float32
BF16 = jnp.bfloat16
ROWS = ("zh", "x", "y")
RANK = ("zl", "core")
COLS = 1024
OWN = 256
SIDE = 128
TILES = COLS // SIDE
LANES = 128
GROUP = 8


def neighbours(x):
    count = lax.axis_size(ROWS)
    up = [(i, i + 1) for i in range(count - 1)]
    down = [(j, i) for i, j in up]
    return lax.ppermute(x, ROWS, up), lax.ppermute(x, ROWS, down)


def pieces_of(x):
    first = lax.reduce_precision(x, 8, 7)
    second = lax.reduce_precision(x - first, 8, 7)
    return [p.astype(BF16)[:, None] for p in (first, second, x - first - second)]


def whole_of(pieces):
    a, b, c = (pieces[i : i + 1, 0].astype(F32) for i in range(3))
    return (a + b) + c


def spread(padded, along_dim, side_weight, centre):
    length = padded.shape[along_dim] - 2
    before = lax.slice_in_dim(padded, 0, length, axis=along_dim)
    middle = lax.slice_in_dim(padded, 1, length + 1, axis=along_dim)
    beyond = lax.slice_in_dim(padded, 2, length + 2, axis=along_dim)
    return side_weight * (before + beyond) + centre * middle


def apply_line(values, along_dim, side_weight, centre):
    widths = [(0, 0)] * values.ndim
    widths[along_dim] = (1, 1)
    return spread(jnp.pad(values, widths), along_dim, side_weight, centre)


def mass_apply(padded):
    result = spread(padded, 1, ONE_SIXTH, 4.0 * ONE_SIXTH)
    result = apply_line(result, 2, ONE_SIXTH, 4.0 * ONE_SIXTH)
    return apply_line(result, 3, ONE_SIXTH, 4.0 * ONE_SIXTH)


def stiff_apply(padded):
    mass_x = spread(padded, 1, ONE_SIXTH, 4.0 * ONE_SIXTH)
    stiff_x = spread(padded, 1, -1.0, 2.0)
    first = apply_line(
        apply_line(stiff_x, 3, ONE_SIXTH, 4.0 * ONE_SIXTH), 2, ONE_SIXTH, 4.0 * ONE_SIXTH
    )
    second = apply_line(apply_line(mass_x, 3, -1.0, 2.0), 2, ONE_SIXTH, 4.0 * ONE_SIXTH)
    third = apply_line(apply_line(mass_x, 3, ONE_SIXTH, 4.0 * ONE_SIXTH), 2, -1.0, 2.0)
    return first + second + third


def halves(x):
    high = x.astype(BF16)
    return high, (x - high.astype(F32)).astype(BF16)

def product(a, b, a_dim=1, b_dim=0):
    dims = (((a_dim,), (b_dim,)), ((), ()))
    def one(p, q):
        return lax.dot_general(p, q, dims, preferred_element_type=F32)
    return one(a[0], b[0]) + (one(a[0], b[1]) + one(a[1], b[0]))

def factor_block(block):
    lane = lax.broadcasted_iota(jnp.int32, (GROUP, SIDE), 1)
    sub = lax.broadcasted_iota(jnp.int32, (GROUP, SIDE), 0)
    count = SIDE // GROUP

    def wide(row):
        return jnp.broadcast_to(row, (GROUP, SIDE))

    def columns(tile, base):
        return [wide(tile[:, base + t : base + t + 1]) for t in range(GROUP)]

    rows = [block[GROUP * v : GROUP * (v + 1), :] for v in range(count)]
    own = columns(rows[0], 0)
    out = []
    for g in range(count):
        base = g * GROUP
        inside = (lane >= base) & (lane < base + GROUP)
        body = jnp.where(inside, 0.0, rows[g])
        pivots = jnp.ones((GROUP, SIDE), F32)
        uppers, inverses, pivot_rows = [], [], []
        for s in range(GROUP):
            pivot = wide(own[s][s : s + 1, :])
            inverse = 1.0 / pivot
            upper = {t: wide(own[t][s : s + 1, :]) for t in range(s + 1, GROUP)}
            taken = jnp.where(sub > s, own[s] * inverse, 0.0)
            pivot_row = jnp.where(lane == base + s, 1.0, wide(body[s : s + 1, :]))
            for t in range(s + 1, GROUP):
                own[t] = own[t] - taken * upper[t]
            body = body - taken * pivot_row
            pivots = jnp.where(sub == s, pivot, pivots)
            uppers.append(upper)
            inverses.append(inverse)
            pivot_rows.append(pivot_row)
        for v in range(g + 1, count):
            cols = columns(rows[v], base)
            new = jnp.where(inside, 0.0, rows[v])
            ahead = columns(rows[v], base + GROUP) if v == g + 1 else []
            for s in range(GROUP):
                taken = cols[s] * inverses[s]
                ahead = [a - taken * wide(cols[s][t : t + 1, :]) for t, a in enumerate(ahead)]
                for t in range(s + 1, GROUP):
                    cols[t] = cols[t] - taken * uppers[s][t]
                new = new - taken * pivot_rows[s]
            rows[v] = new
            own = ahead or own
        low = jnp.where(lane == sub + base, 1.0, jnp.where(lane < base + GROUP, body, 0.0))
        scale = lax.rsqrt(pivots)
        scale = scale * (1.5 - 0.5 * pivots * scale * scale)
        out.append(low * scale)
    return jnp.concatenate(out, axis=0)


def factor_kernel(where, left, right, left_other, right_other, inv_out, proj_out, high, low, m, r_high, r_low):
    core = where[1]
    strip = OWN // 4

    def load(r, squares):
        inner = pl.ds(pl.multiple_of(r * strip, strip), strip)
        for half, pair in enumerate(((left, left_other), (right, right_other))):
            for chip in range(2):
                for other, source in enumerate(pair):
                    block = chip * 2 + (core if other == 0 else 1 - core)
                    lanes = pl.ds(pl.multiple_of(block * OWN + half * LANES, LANES), LANES)
                    x = source[chip, inner, :]
                    for at in range(0, strip, GROUP):
                        squares = squares + x[at : at + GROUP] * x[at : at + GROUP]
                    upper, lower = halves(x)
                    target = (block ^ (r // 4)) * OWN + (r % 4) * strip
                    rows = pl.ds(pl.multiple_of(target, strip), strip)
                    high[rows, lanes] = upper
                    low[rows, lanes] = lower
        return squares

    squares = lax.fori_loop(0, COLS // strip, load, jnp.zeros((GROUP, LANES), F32))
    total = jnp.sum(jnp.sum(squares, axis=0, keepdims=True), axis=1, keepdims=True)
    level = total / COLS + 1e-6
    scale = 1.0 / level
    eye = (lax.broadcasted_iota(jnp.int32, (SIDE, SIDE), 0) == lax.broadcasted_iota(jnp.int32, (SIDE, SIDE), 1)).astype(F32)
    def gram(a, carry):
        left_rows = pl.ds(pl.multiple_of(a * OWN, OWN), OWN)

        def one(b, inner):
            right_rows = pl.ds(pl.multiple_of(b * OWN, OWN), OWN)
            pair = product(
                (high[left_rows, :], low[left_rows, :]),
                (high[right_rows, :], low[right_rows, :]),
                1,
                1,
            )
            m[left_rows, right_rows] = pair * scale
            return inner

        return lax.fori_loop(a, COLS // OWN, one, carry)

    lax.fori_loop(0, COLS // OWN, gram, 0)

    def step(k, carry):
        block = pl.ds(pl.multiple_of(k * SIDE, SIDE), SIDE)
        x = factor_block(m[block, block] + eye)
        m[block, block] = eye
        r = product(halves(x), halves(m[block, :]))
        m[block, :] = r
        upper, lower = halves(r)
        r_high[...] = upper
        r_low[...] = lower

        def update(i, inner):
            rows = pl.ds(pl.multiple_of(i * SIDE, SIDE), SIDE)
            m[rows, block] = jnp.zeros((SIDE, SIDE), F32)
            mine = (r_high[:, rows], r_low[:, rows])
            m[rows, :] = m[rows, :] - product(mine, (r_high[...], r_low[...]), 0, 0)
            return inner

        lax.fori_loop(k + 1, TILES, update, 0)
        return carry

    lax.fori_loop(0, TILES, step, 0)
    first = pl.multiple_of(where[0] * OWN, OWN)
    row = lax.broadcasted_iota(jnp.int32, (OWN, OWN), 0)
    column = lax.broadcasted_iota(jnp.int32, (OWN, OWN), 1)
    own = []
    for block in range(4):
        part = m[pl.ds(first, OWN), block * OWN : (block + 1) * OWN]
        own.append(jnp.where(column + block * OWN <= row + first, part, 0.0))
    own = halves(jnp.concatenate(own, axis=1))
    shrink = lax.rsqrt(level)
    def project(turn, carry):
        block = where[0] ^ turn
        lanes = pl.ds(pl.multiple_of(block * OWN, OWN), OWN)
        out = pl.ds(pl.multiple_of(turn * OWN, OWN), OWN)
        part = m[pl.ds(first, OWN), lanes]
        part = jnp.where(column + block * OWN <= row + first, part, 0.0)
        inv_out[:, out] = part.astype(BF16)
        proj_out[:, out] = (product(own, (high[:, lanes], low[:, lanes])) * shrink).astype(BF16)
        return carry

    lax.fori_loop(0, 4, project, 0)


def factor(where, left, right, left_other, right_other):
    vmem = pl.BlockSpec(memory_space=pltpu.VMEM)
    return pl.pallas_call(
        factor_kernel,
        out_shape=(jax.ShapeDtypeStruct((OWN, COLS), BF16),) * 2,
        in_specs=[pl.BlockSpec(memory_space=pltpu.SMEM)] + [vmem] * 4,
        out_specs=[vmem] * 2,
        scratch_shapes=[
            pltpu.VMEM((COLS, COLS), BF16),
            pltpu.VMEM((COLS, COLS), BF16),
            pltpu.VMEM((COLS, COLS), F32),
            pltpu.VMEM((SIDE, COLS), BF16),
            pltpu.VMEM((SIDE, COLS), BF16),
        ],
        compiler_params=pltpu.CompilerParams(vmem_limit_bytes=20 * 2**20),
    )(where, left, right, left_other, right_other)


def gather_four(x, axis, dim):
    here = lax.axis_index(axis)
    shape = list(x.shape)
    shape[dim] = 4
    full = lax.dynamic_update_slice_in_dim(jnp.zeros(shape, x.dtype), x, here, dim)
    for step in (1, 2, 3):
        moved = lax.ppermute(x, axis, [(d, (d + step) % 4) for d in range(4)])
        full = lax.dynamic_update_slice_in_dim(full, moved, (here - step) % 4, dim)
    return full


def turned(x):
    moved = [lax.ppermute(x, RANK, [(d, d ^ step) for d in range(4)]) for step in (1, 2, 3)]
    return jnp.concatenate([x] + moved, axis=0)


SWAP = [(0, 1), (1, 0)]


def relayed(x, across, axis):
    near = lax.ppermute(x, "core", SWAP)
    return jnp.concatenate([x, near, across, lax.ppermute(across, "core", SWAP)], axis=axis)


def replane(observe):
    columns, depth, own, _ = observe.shape
    planes = jnp.transpose(observe, (3, 2, 1, 0)).reshape(4, 16, own, depth, columns)
    here = lax.axis_index("zh")
    held = jnp.zeros((16, 4, own, depth, columns), observe.dtype)
    held = lax.dynamic_update_slice_in_dim(
        held, lax.dynamic_index_in_dim(planes, here, 0, False)[:, None], here, 1
    )
    for step in (1, 2, 3):
        leaving = lax.dynamic_index_in_dim(planes, (here + step) % 4, 0, False)
        came = lax.ppermute(leaving, "zh", [(d, (d + step) % 4) for d in range(4)])
        held = lax.dynamic_update_slice_in_dim(held, came[:, None], (here - step) % 4, 1)
    held = lax.all_to_all(held, ("x", "y"), split_axis=0, concat_axis=0, tiled=True)
    return jnp.transpose(held, (3, 1, 0, 2, 4)).reshape(depth * 4 * 16 * own, columns)


def body(control, observe, capacity, conduct):
    col_rows = control.shape[0]
    local_cells = control.shape[1] * control.shape[2] * control.shape[3]
    packed = jnp.concatenate([control] + pieces_of(capacity) + pieces_of(conduct), axis=0)
    before, after = neighbours(packed)
    relaid = replane(observe)
    before, after, relaid = lax.optimization_barrier((before, after, relaid))
    at = col_rows + 3
    capacities = jnp.concatenate(
        [whole_of(before[col_rows:at]), capacity, whole_of(after[col_rows:at])], axis=0
    )
    conducts = jnp.concatenate([whole_of(before[at:]), conduct, whole_of(after[at:])], axis=0)
    control_wide = jnp.concatenate([before[:col_rows], control, after[:col_rows]], axis=1)
    widened = (capacities * control_wide.astype(F32)).astype(BF16)
    applied = (capacity * mass_apply(widened.astype(F32))).astype(BF16)
    applied_flat = applied.reshape(col_rows, local_cells)
    applied_all = relayed(applied_flat, lax.ppermute(applied_flat, "zl", SWAP), 0)
    part = jnp.dot(applied_all, relaid, preferred_element_type=F32)
    relaid, part = lax.optimization_barrier((relaid, part))
    across = lax.ppermute(relaid, "zl", SWAP)
    pieces = lax.all_to_all(part, ("x", "y"), split_axis=0, concat_axis=0, tiled=True)
    pieces, across = lax.optimization_barrier((pieces, across))
    relaid_all = relayed(relaid, across, 1)
    chunk = jnp.sum(pieces.reshape(16, COLS // 16, OWN), axis=0)
    summed = chunk
    for step in (1, 2, 3):
        summed = summed + lax.ppermute(chunk, "zh", [(d, (d + step) % 4) for d in range(4)])
    low = lax.axis_index("zl") == 0
    other = lax.ppermute(summed, "zl", SWAP)
    pair = jnp.stack([jnp.where(low, summed, other), jnp.where(low, other, summed)])
    pair = pair.reshape(2, 1, 1, COLS // 16, OWN)
    control_flat = control_wide.reshape(col_rows, 3 * local_cells)
    control_flat, pair = lax.optimization_barrier((control_flat, pair))
    control_all = turned(control_flat)
    left_half = gather_four(pair[..., :LANES], "x", 1)
    right_half = gather_four(pair[..., LANES:], "y", 2)
    left_half = gather_four(left_half, "y", 2).reshape(2, COLS, LANES)
    right_half = gather_four(right_half, "x", 1).reshape(2, COLS, LANES)
    left_other = lax.ppermute(left_half, "core", SWAP)
    right_other = lax.ppermute(right_half, "core", SWAP)
    where = jnp.stack([lax.axis_index(RANK), lax.axis_index("core")]).astype(jnp.int32)
    inverse_low, project_low = factor(where, left_half, right_half, left_other, right_other)
    right_basis = jnp.dot(inverse_low, control_all, preferred_element_type=F32)
    right_basis = right_basis.reshape(control_wide.shape)
    scaled_right = (conducts * right_basis).astype(BF16)
    stiff_basis = (-(conduct * stiff_apply(scaled_right.astype(F32)))).astype(BF16)
    left_sum = lax.dot_general(
        project_low, relaid_all, (((1,), (1,)), ((), ())), preferred_element_type=F32
    )
    left_basis = left_sum.astype(BF16).reshape(control.shape)
    return (left_basis, stiff_basis)


def solution(mesh):
    torus = Mesh(mesh.devices.reshape(4, 4, 4, 2, 2), ROWS + RANK)
    in_specs = (
        P(RANK, ROWS, None, None),
        P(RANK, None, ROWS, None),
        P(ROWS, None, None),
        P(ROWS, None, None),
    )
    out_specs = (P(RANK, ROWS, None, None), P(RANK, ROWS, None, None))
    return jax.shard_map(body, mesh=torus, in_specs=in_specs, out_specs=out_specs, check_vma=False)
```

```python
import jax
import jax.numpy as jnp
from jax import lax
from jax.experimental import pallas as pl
from jax.experimental.pallas import tpu as pltpu
from jax.sharding import Mesh
from jax.sharding import PartitionSpec as P


ONE_SIXTH = 1.0 / 6.0
F32 = jnp.float32
BF16 = jnp.bfloat16
ROWS = ("zh", "x", "y")
RANK = ("zl", "core")
COLS = 1024
OWN = 256
SIDE = 128
TILES = COLS // SIDE
LANES = 128
GROUP = 8


def neighbours(x):
    count = lax.axis_size(ROWS)
    up = [(i, i + 1) for i in range(count - 1)]
    down = [(j, i) for i, j in up]
    return lax.ppermute(x, ROWS, up), lax.ppermute(x, ROWS, down)


def pieces_of(x):
    first = lax.reduce_precision(x, 8, 7)
    second = lax.reduce_precision(x - first, 8, 7)
    return [p.astype(BF16)[:, None] for p in (first, second, x - first - second)]


def whole_of(pieces):
    a, b, c = (pieces[i : i + 1, 0].astype(F32) for i in range(3))
    return (a + b) + c


def spread(padded, along_dim, side_weight, centre):
    length = padded.shape[along_dim] - 2
    before = lax.slice_in_dim(padded, 0, length, axis=along_dim)
    middle = lax.slice_in_dim(padded, 1, length + 1, axis=along_dim)
    beyond = lax.slice_in_dim(padded, 2, length + 2, axis=along_dim)
    return side_weight * (before + beyond) + centre * middle


def apply_line(values, along_dim, side_weight, centre):
    widths = [(0, 0)] * values.ndim
    widths[along_dim] = (1, 1)
    return spread(jnp.pad(values, widths), along_dim, side_weight, centre)


def mass_apply(padded):
    result = spread(padded, 1, ONE_SIXTH, 4.0 * ONE_SIXTH)
    result = apply_line(result, 2, ONE_SIXTH, 4.0 * ONE_SIXTH)
    return apply_line(result, 3, ONE_SIXTH, 4.0 * ONE_SIXTH)


def stiff_apply(padded):
    mass_x = spread(padded, 1, ONE_SIXTH, 4.0 * ONE_SIXTH)
    stiff_x = spread(padded, 1, -1.0, 2.0)
    first = apply_line(
        apply_line(stiff_x, 3, ONE_SIXTH, 4.0 * ONE_SIXTH), 2, ONE_SIXTH, 4.0 * ONE_SIXTH
    )
    second = apply_line(apply_line(mass_x, 3, -1.0, 2.0), 2, ONE_SIXTH, 4.0 * ONE_SIXTH)
    third = apply_line(apply_line(mass_x, 3, ONE_SIXTH, 4.0 * ONE_SIXTH), 2, -1.0, 2.0)
    return first + second + third


def halves(x):
    high = x.astype(BF16)
    return high, (x - high.astype(F32)).astype(BF16)

def product(a, b, a_dim=1, b_dim=0):
    dims = (((a_dim,), (b_dim,)), ((), ()))
    def one(p, q):
        return lax.dot_general(p, q, dims, preferred_element_type=F32)
    return one(a[0], b[0]) + (one(a[0], b[1]) + one(a[1], b[0]))

def factor_block(block):
    lane = lax.broadcasted_iota(jnp.int32, (GROUP, SIDE), 1)
    sub = lax.broadcasted_iota(jnp.int32, (GROUP, SIDE), 0)
    count = SIDE // GROUP

    def wide(row):
        return jnp.broadcast_to(row, (GROUP, SIDE))

    def columns(tile, base):
        return [wide(tile[:, base + t : base + t + 1]) for t in range(GROUP)]

    rows = [block[GROUP * v : GROUP * (v + 1), :] for v in range(count)]
    own = columns(rows[0], 0)
    out = []
    for g in range(count):
        base = g * GROUP
        inside = (lane >= base) & (lane < base + GROUP)
        body = jnp.where(inside, 0.0, rows[g])
        pivots = jnp.ones((GROUP, SIDE), F32)
        uppers, inverses, pivot_rows = [], [], []
        for s in range(GROUP):
            pivot = wide(own[s][s : s + 1, :])
            inverse = 1.0 / pivot
            upper = {t: wide(own[t][s : s + 1, :]) for t in range(s + 1, GROUP)}
            taken = jnp.where(sub > s, own[s] * inverse, 0.0)
            pivot_row = jnp.where(lane == base + s, 1.0, wide(body[s : s + 1, :]))
            for t in range(s + 1, GROUP):
                own[t] = own[t] - taken * upper[t]
            body = body - taken * pivot_row
            pivots = jnp.where(sub == s, pivot, pivots)
            uppers.append(upper)
            inverses.append(inverse)
            pivot_rows.append(pivot_row)
        for v in range(g + 1, count):
            cols = columns(rows[v], base)
            new = jnp.where(inside, 0.0, rows[v])
            ahead = columns(rows[v], base + GROUP) if v == g + 1 else []
            for s in range(GROUP):
                taken = cols[s] * inverses[s]
                ahead = [a - taken * wide(cols[s][t : t + 1, :]) for t, a in enumerate(ahead)]
                for t in range(s + 1, GROUP):
                    cols[t] = cols[t] - taken * uppers[s][t]
                new = new - taken * pivot_rows[s]
            rows[v] = new
            own = ahead or own
        low = jnp.where(lane == sub + base, 1.0, jnp.where(lane < base + GROUP, body, 0.0))
        scale = lax.rsqrt(pivots)
        scale = scale * (1.5 - 0.5 * pivots * scale * scale)
        out.append(low * scale)
    return jnp.concatenate(out, axis=0)


def factor_kernel(where, left, right, left_other, right_other, inv_out, proj_out, high, low, m, r_high, r_low):
    core = where[1]
    strip = OWN // 4

    def load(r, squares):
        inner = pl.ds(pl.multiple_of(r * strip, strip), strip)
        for half, pair in enumerate(((left, left_other), (right, right_other))):
            for chip in range(2):
                for other, source in enumerate(pair):
                    block = chip * 2 + (core if other == 0 else 1 - core)
                    lanes = pl.ds(pl.multiple_of(block * OWN + half * LANES, LANES), LANES)
                    x = source[chip, inner, :]
                    for at in range(0, strip, GROUP):
                        squares = squares + x[at : at + GROUP] * x[at : at + GROUP]
                    upper, lower = halves(x)
                    target = (block ^ (r // 4)) * OWN + (r % 4) * strip
                    rows = pl.ds(pl.multiple_of(target, strip), strip)
                    high[rows, lanes] = upper
                    low[rows, lanes] = lower
        return squares

    squares = lax.fori_loop(0, COLS // strip, load, jnp.zeros((GROUP, LANES), F32))
    total = jnp.sum(jnp.sum(squares, axis=0, keepdims=True), axis=1, keepdims=True)
    level = total / COLS + 1e-6
    scale = 1.0 / level
    eye = (lax.broadcasted_iota(jnp.int32, (SIDE, SIDE), 0) == lax.broadcasted_iota(jnp.int32, (SIDE, SIDE), 1)).astype(F32)
    def gram(a, carry):
        left_rows = pl.ds(pl.multiple_of(a * OWN, OWN), OWN)

        def one(b, inner):
            right_rows = pl.ds(pl.multiple_of(b * OWN, OWN), OWN)
            pair = product(
                (high[left_rows, :], low[left_rows, :]),
                (high[right_rows, :], low[right_rows, :]),
                1,
                1,
            )
            m[left_rows, right_rows] = pair * scale
            return inner

        return lax.fori_loop(a, COLS // OWN, one, carry)

    lax.fori_loop(0, COLS // OWN, gram, 0)

    def step(k, carry):
        block = pl.ds(pl.multiple_of(k * SIDE, SIDE), SIDE)
        x = factor_block(m[block, block] + eye)
        m[block, block] = eye
        r = product(halves(x), halves(m[block, :]))
        m[block, :] = r
        upper, lower = halves(r)
        r_high[...] = upper
        r_low[...] = lower

        def update(i, inner):
            rows = pl.ds(pl.multiple_of(i * SIDE, SIDE), SIDE)
            m[rows, block] = jnp.zeros((SIDE, SIDE), F32)
            mine = (r_high[:, rows], r_low[:, rows])
            m[rows, :] = m[rows, :] - product(mine, (r_high[...], r_low[...]), 0, 0)
            return inner

        lax.fori_loop(k + 1, TILES, update, 0)
        return carry

    lax.fori_loop(0, TILES, step, 0)
    first = pl.multiple_of(where[0] * OWN, OWN)
    row = lax.broadcasted_iota(jnp.int32, (OWN, OWN), 0)
    column = lax.broadcasted_iota(jnp.int32, (OWN, OWN), 1)
    own = []
    for block in range(4):
        part = m[pl.ds(first, OWN), block * OWN : (block + 1) * OWN]
        own.append(jnp.where(column + block * OWN <= row + first, part, 0.0))
    own = halves(jnp.concatenate(own, axis=1))
    shrink = lax.rsqrt(level)
    def project(turn, carry):
        block = where[0] ^ turn
        lanes = pl.ds(pl.multiple_of(block * OWN, OWN), OWN)
        out = pl.ds(pl.multiple_of(turn * OWN, OWN), OWN)
        part = m[pl.ds(first, OWN), lanes]
        part = jnp.where(column + block * OWN <= row + first, part, 0.0)
        inv_out[:, out] = part.astype(BF16)
        proj_out[:, out] = (product(own, (high[:, lanes], low[:, lanes])) * shrink).astype(BF16)
        return carry

    lax.fori_loop(0, 4, project, 0)


def factor(where, left, right, left_other, right_other):
    vmem = pl.BlockSpec(memory_space=pltpu.VMEM)
    return pl.pallas_call(
        factor_kernel,
        out_shape=(jax.ShapeDtypeStruct((OWN, COLS), BF16),) * 2,
        in_specs=[pl.BlockSpec(memory_space=pltpu.SMEM)] + [vmem] * 4,
        out_specs=[vmem] * 2,
        scratch_shapes=[
            pltpu.VMEM((COLS, COLS), BF16),
            pltpu.VMEM((COLS, COLS), BF16),
            pltpu.VMEM((COLS, COLS), F32),
            pltpu.VMEM((SIDE, COLS), BF16),
            pltpu.VMEM((SIDE, COLS), BF16),
        ],
        compiler_params=pltpu.CompilerParams(vmem_limit_bytes=20 * 2**20),
    )(where, left, right, left_other, right_other)


def gather_four(x, axis, dim):
    here = lax.axis_index(axis)
    shape = list(x.shape)
    shape[dim] = 4
    full = lax.dynamic_update_slice_in_dim(jnp.zeros(shape, x.dtype), x, here, dim)
    for step in (1, 2, 3):
        moved = lax.ppermute(x, axis, [(d, (d + step) % 4) for d in range(4)])
        full = lax.dynamic_update_slice_in_dim(full, moved, (here - step) % 4, dim)
    return full


def turned(x):
    moved = [lax.ppermute(x, RANK, [(d, d ^ step) for d in range(4)]) for step in (1, 2, 3)]
    return jnp.concatenate([x] + moved, axis=0)


SWAP = [(0, 1), (1, 0)]


def relayed(x, across, axis):
    near = lax.ppermute(x, "core", SWAP)
    return jnp.concatenate([x, near, across, lax.ppermute(across, "core", SWAP)], axis=axis)


def replane(observe, waiting):
    columns, depth, own, _ = observe.shape
    planes = jnp.transpose(observe.reshape(columns, depth, own, 4, 16), (4, 3, 2, 1, 0))
    planes = lax.all_to_all(planes, ("x", "y"), split_axis=0, concat_axis=0, tiled=True)
    here = lax.axis_index("zh")
    held = jnp.zeros((4, 16, own, depth, columns), observe.dtype)
    held = lax.dynamic_update_slice_in_dim(
        held, lax.dynamic_index_in_dim(planes, here, 1, False)[None], here, 0
    )
    came = []
    for step in (1, 2, 3):
        leaving = lax.dynamic_index_in_dim(planes, (here + step) % 4, 1, False)
        came.append(lax.ppermute(leaving, "zh", [(d, (d + step) % 4) for d in range(4)]))
    *came, before, after = lax.optimization_barrier((*came, *waiting))
    for step in (1, 2, 3):
        held = lax.dynamic_update_slice_in_dim(held, came[step - 1][None], (here - step) % 4, 0)
    return jnp.transpose(held, (3, 0, 1, 2, 4)).reshape(depth * 64 * own, columns), (before, after)


def rounded(x):
    return lax.reduce_precision(x, 8, 7).astype(BF16)


def body(control, observe, capacity, conduct):
    col_rows = control.shape[0]
    local_cells = control.shape[1] * control.shape[2] * control.shape[3]
    small = jnp.concatenate(pieces_of(capacity) + pieces_of(conduct), axis=0)
    packed = jnp.concatenate([control, lax.optimization_barrier(small)], axis=0)
    before, after = neighbours(packed)
    relaid, (before, after) = replane(observe, (before, after))
    at = col_rows + 3
    capacities = jnp.concatenate(
        [whole_of(before[col_rows:at]), capacity, whole_of(after[col_rows:at])], axis=0
    )
    conducts = jnp.concatenate([whole_of(before[at:]), conduct, whole_of(after[at:])], axis=0)
    control_wide = jnp.concatenate([before[:col_rows], control, after[:col_rows]], axis=1)
    widened = rounded(capacities * control_wide.astype(F32))
    applied = (capacity * mass_apply(widened.astype(F32))).astype(BF16)
    applied_flat = applied.reshape(col_rows, local_cells)
    applied_all = relayed(applied_flat, lax.ppermute(applied_flat, "zl", SWAP), 0)
    part = jnp.dot(applied_all, relaid, preferred_element_type=F32)
    relaid, part = lax.optimization_barrier((relaid, part))
    across = lax.ppermute(relaid, "zl", SWAP)
    pieces = lax.all_to_all(part, ("x", "y"), split_axis=0, concat_axis=0, tiled=True)
    pieces, across = lax.optimization_barrier((pieces, across))
    relaid_all = relayed(relaid, across, 1)
    chunk = jnp.sum(pieces.reshape(16, COLS // 16, OWN), axis=0)
    spread_out = jnp.broadcast_to(chunk, (8, COLS // 16, OWN))
    pair = lax.all_to_all(spread_out, ("zh", "zl"), split_axis=0, concat_axis=0, tiled=True)
    pair = jnp.sum(pair.reshape(4, 2, COLS // 16, OWN), axis=0)
    pair = pair.reshape(2, 1, 1, COLS // 16, OWN)
    control_flat = control_wide.reshape(col_rows, 3 * local_cells)
    control_flat, pair = lax.optimization_barrier((control_flat, pair))
    control_all = turned(control_flat)
    left_half = gather_four(pair[..., :LANES], "x", 1)
    right_half = gather_four(pair[..., LANES:], "y", 2)
    left_half = gather_four(left_half, "y", 2).reshape(2, COLS, LANES)
    right_half = gather_four(right_half, "x", 1).reshape(2, COLS, LANES)
    left_other = lax.ppermute(left_half, "core", SWAP)
    right_other = lax.ppermute(right_half, "core", SWAP)
    where = jnp.stack([lax.axis_index(RANK), lax.axis_index("core")]).astype(jnp.int32)
    inverse_low, project_low = factor(where, left_half, right_half, left_other, right_other)
    right_basis = jnp.dot(inverse_low, control_all, preferred_element_type=F32)
    right_basis = right_basis.reshape(control_wide.shape)
    scaled_right = rounded(conducts * right_basis)
    stiff_basis = (-(conduct * stiff_apply(scaled_right.astype(F32)))).astype(BF16)
    left_sum = lax.dot_general(
        project_low, relaid_all, (((1,), (1,)), ((), ())), preferred_element_type=F32
    )
    left_basis = left_sum.astype(BF16).reshape(control.shape)
    return (left_basis, stiff_basis)


def solution(mesh):
    torus = Mesh(mesh.devices.reshape(4, 4, 4, 2, 2), ROWS + RANK)
    in_specs = (
        P(RANK, ROWS, None, None),
        P(RANK, None, ROWS, None),
        P(ROWS, None, None),
        P(ROWS, None, None),
    )
    out_specs = (P(RANK, ROWS, None, None), P(RANK, ROWS, None, None))
    return jax.shard_map(body, mesh=torus, in_specs=in_specs, out_specs=out_specs, check_vma=False)
```

```python
import jax
import jax.numpy as jnp
from jax import lax
from jax.experimental import pallas as pl
from jax.experimental.pallas import tpu as pltpu
from jax.sharding import Mesh
from jax.sharding import PartitionSpec as P


ONE_SIXTH = 1.0 / 6.0
F32 = jnp.float32
BF16 = jnp.bfloat16
ROWS = ("zh", "x", "y")
RANK = ("zl", "core")
COLS = 1024
OWN = 256
SIDE = 128
TILES = COLS // SIDE
LANES = 128
GROUP = 8


def neighbours(x):
    count = lax.axis_size(ROWS)
    up = [(i, i + 1) for i in range(count - 1)]
    down = [(j, i) for i, j in up]
    before = lax.ppermute(x, ROWS, up)
    after = lax.ppermute(x, ROWS, down)
    return before, after


def spread(padded, along_dim, side_weight, centre):
    length = padded.shape[along_dim] - 2
    before = lax.slice_in_dim(padded, 0, length, axis=along_dim)
    middle = lax.slice_in_dim(padded, 1, length + 1, axis=along_dim)
    beyond = lax.slice_in_dim(padded, 2, length + 2, axis=along_dim)
    return side_weight * (before + beyond) + centre * middle


def apply_line(values, along_dim, side_weight, centre):
    widths = [(0, 0)] * values.ndim
    widths[along_dim] = (1, 1)
    return spread(jnp.pad(values, widths), along_dim, side_weight, centre)


def mass_apply(padded):
    result = spread(padded, 1, ONE_SIXTH, 4.0 * ONE_SIXTH)
    result = apply_line(result, 2, ONE_SIXTH, 4.0 * ONE_SIXTH)
    return apply_line(result, 3, ONE_SIXTH, 4.0 * ONE_SIXTH)


def stiff_apply(padded):
    mass_x = spread(padded, 1, ONE_SIXTH, 4.0 * ONE_SIXTH)
    stiff_x = spread(padded, 1, -1.0, 2.0)
    first = apply_line(
        apply_line(stiff_x, 3, ONE_SIXTH, 4.0 * ONE_SIXTH), 2, ONE_SIXTH, 4.0 * ONE_SIXTH
    )
    second = apply_line(apply_line(mass_x, 3, -1.0, 2.0), 2, ONE_SIXTH, 4.0 * ONE_SIXTH)
    third = apply_line(apply_line(mass_x, 3, ONE_SIXTH, 4.0 * ONE_SIXTH), 2, -1.0, 2.0)
    return first + second + third


def halves(x):
    high = x.astype(BF16)
    return high, (x - high.astype(F32)).astype(BF16)


def product(a, b, a_dim=1, b_dim=0):
    dims = (((a_dim,), (b_dim,)), ((), ()))

    def one(p, q):
        return lax.dot_general(p, q, dims, preferred_element_type=F32)

    return one(a[0], b[0]) + (one(a[0], b[1]) + one(a[1], b[0]))


def factor_block(block):
    lane = lax.broadcasted_iota(jnp.int32, (GROUP, SIDE), 1)
    sub = lax.broadcasted_iota(jnp.int32, (GROUP, SIDE), 0)
    count = SIDE // GROUP

    def wide(row):
        return jnp.broadcast_to(row, (GROUP, SIDE))

    def columns(tile, base):
        return [wide(tile[:, base + t : base + t + 1]) for t in range(GROUP)]

    rows = [block[GROUP * v : GROUP * (v + 1), :] for v in range(count)]
    own = columns(rows[0], 0)
    out = []
    for g in range(count):
        base = g * GROUP
        inside = (lane >= base) & (lane < base + GROUP)
        body = jnp.where(inside, 0.0, rows[g])
        pivots = jnp.ones((GROUP, SIDE), F32)
        uppers, inverses, pivot_rows = [], [], []
        for s in range(GROUP):
            pivot = wide(own[s][s : s + 1, :])
            inverse = 1.0 / pivot
            upper = {t: wide(own[t][s : s + 1, :]) for t in range(s + 1, GROUP)}
            taken = jnp.where(sub > s, own[s] * inverse, 0.0)
            pivot_row = jnp.where(lane == base + s, 1.0, wide(body[s : s + 1, :]))
            for t in range(s + 1, GROUP):
                own[t] = own[t] - taken * upper[t]
            body = body - taken * pivot_row
            pivots = jnp.where(sub == s, pivot, pivots)
            uppers.append(upper)
            inverses.append(inverse)
            pivot_rows.append(pivot_row)
        for v in range(g + 1, count):
            cols = columns(rows[v], base)
            new = jnp.where(inside, 0.0, rows[v])
            ahead = columns(rows[v], base + GROUP) if v == g + 1 else []
            for s in range(GROUP):
                taken = cols[s] * inverses[s]
                ahead = [a - taken * wide(cols[s][t : t + 1, :]) for t, a in enumerate(ahead)]
                for t in range(s + 1, GROUP):
                    cols[t] = cols[t] - taken * uppers[s][t]
                new = new - taken * pivot_rows[s]
            rows[v] = new
            own = ahead or own
        low = jnp.where(lane == sub + base, 1.0, jnp.where(lane < base + GROUP, body, 0.0))
        scale = lax.rsqrt(pivots)
        scale = scale * (1.5 - 0.5 * pivots * scale * scale)
        out.append(low * scale)
    return jnp.concatenate(out, axis=0)


def factor_kernel(where, left, right, left_other, right_other, inv_out, proj_out, high, low, m, r_high, r_low):
    core = where[1]
    strip = OWN // 4

    def load(r, squares):
        inner = pl.ds(pl.multiple_of(r * strip, strip), strip)
        for half, pair in enumerate(((left, left_other), (right, right_other))):
            for chip in range(2):
                for other, source in enumerate(pair):
                    block = chip * 2 + (core if other == 0 else 1 - core)
                    lanes = pl.ds(pl.multiple_of(block * OWN + half * LANES, LANES), LANES)
                    x = source[chip, inner, :]
                    for at in range(0, strip, GROUP):
                        squares = squares + x[at : at + GROUP] * x[at : at + GROUP]
                    upper, lower = halves(x)
                    target = (block ^ (r // 4)) * OWN + (r % 4) * strip
                    rows = pl.ds(pl.multiple_of(target, strip), strip)
                    high[rows, lanes] = upper
                    low[rows, lanes] = lower
        return squares

    squares = lax.fori_loop(0, COLS // strip, load, jnp.zeros((GROUP, LANES), F32))
    total = jnp.sum(jnp.sum(squares, axis=0, keepdims=True), axis=1, keepdims=True)
    level = total / COLS + 1e-6
    scale = 1.0 / level
    eye = (lax.broadcasted_iota(jnp.int32, (SIDE, SIDE), 0) == lax.broadcasted_iota(jnp.int32, (SIDE, SIDE), 1)).astype(F32)

    def gram(a, carry):
        left_rows = pl.ds(pl.multiple_of(a * OWN, OWN), OWN)

        def one(b, inner):
            right_rows = pl.ds(pl.multiple_of(b * OWN, OWN), OWN)
            pair = product(
                (high[left_rows, :], low[left_rows, :]),
                (high[right_rows, :], low[right_rows, :]),
                1,
                1,
            )
            m[left_rows, right_rows] = pair * scale
            return inner

        return lax.fori_loop(a, COLS // OWN, one, carry)

    lax.fori_loop(0, COLS // OWN, gram, 0)

    def step(k, carry):
        block = pl.ds(pl.multiple_of(k * SIDE, SIDE), SIDE)
        x = factor_block(m[block, block] + eye)
        m[block, block] = eye
        r = product(halves(x), halves(m[block, :]))
        m[block, :] = r
        upper, lower = halves(r)
        r_high[...] = upper
        r_low[...] = lower

        def update(i, inner):
            rows = pl.ds(pl.multiple_of(i * SIDE, SIDE), SIDE)
            m[rows, block] = jnp.zeros((SIDE, SIDE), F32)
            mine = (r_high[:, rows], r_low[:, rows])
            m[rows, :] = m[rows, :] - product(mine, (r_high[...], r_low[...]), 0, 0)
            return inner

        lax.fori_loop(k + 1, TILES, update, 0)
        return carry

    lax.fori_loop(0, TILES, step, 0)
    first = pl.multiple_of(where[0] * OWN, OWN)
    row = lax.broadcasted_iota(jnp.int32, (OWN, OWN), 0)
    column = lax.broadcasted_iota(jnp.int32, (OWN, OWN), 1)
    own = []
    for block in range(4):
        part = m[pl.ds(first, OWN), block * OWN : (block + 1) * OWN]
        own.append(jnp.where(column + block * OWN <= row + first, part, 0.0))
    own = halves(jnp.concatenate(own, axis=1))
    shrink = lax.rsqrt(level)

    def project(turn, carry):
        block = where[0] ^ turn
        lanes = pl.ds(pl.multiple_of(block * OWN, OWN), OWN)
        out = pl.ds(pl.multiple_of(turn * OWN, OWN), OWN)
        part = m[pl.ds(first, OWN), lanes]
        part = jnp.where(column + block * OWN <= row + first, part, 0.0)
        inv_out[:, out] = part.astype(BF16)
        proj_out[:, out] = (product(own, (high[:, lanes], low[:, lanes])) * shrink).astype(BF16)
        return carry

    lax.fori_loop(0, 4, project, 0)


def factor(where, left, right, left_other, right_other):
    vmem = pl.BlockSpec(memory_space=pltpu.VMEM)
    return pl.pallas_call(
        factor_kernel,
        out_shape=(jax.ShapeDtypeStruct((OWN, COLS), BF16),) * 2,
        in_specs=[pl.BlockSpec(memory_space=pltpu.SMEM)] + [vmem] * 4,
        out_specs=[vmem] * 2,
        scratch_shapes=[
            pltpu.VMEM((COLS, COLS), BF16),
            pltpu.VMEM((COLS, COLS), BF16),
            pltpu.VMEM((COLS, COLS), F32),
            pltpu.VMEM((SIDE, COLS), BF16),
            pltpu.VMEM((SIDE, COLS), BF16),
        ],
        compiler_params=pltpu.CompilerParams(vmem_limit_bytes=20 * 2**20),
    )(where, left, right, left_other, right_other)


def gather_four(x, axis, dim):
    here = lax.axis_index(axis)
    shape = list(x.shape)
    shape[dim] = 4
    full = lax.dynamic_update_slice_in_dim(jnp.zeros(shape, x.dtype), x, here, dim)
    for step in (1, 2, 3):
        moved = lax.ppermute(x, axis, [(d, (d + step) % 4) for d in range(4)])
        full = lax.dynamic_update_slice_in_dim(full, moved, (here - step) % 4, dim)
    return full


def turned(x):
    moved = [lax.ppermute(x, RANK, [(d, d ^ step) for d in range(4)]) for step in (1, 2, 3)]
    return jnp.concatenate([x] + moved, axis=0)


SWAP = [(0, 1), (1, 0)]


def relayed(x, across, axis):
    near = lax.ppermute(x, "core", SWAP)
    return jnp.concatenate([x, near, across, lax.ppermute(across, "core", SWAP)], axis=axis)


def replane(observe):
    columns, depth, own, _ = observe.shape
    planes = jnp.transpose(observe.reshape(columns, depth, own, 4, 16), (4, 3, 2, 1, 0))
    planes = lax.all_to_all(planes, ("x", "y"), split_axis=0, concat_axis=0, tiled=True)
    here = lax.axis_index("zh")
    held = jnp.zeros((4, 16, own, depth, columns), observe.dtype)
    held = lax.dynamic_update_slice_in_dim(
        held, lax.dynamic_index_in_dim(planes, here, 1, False)[None], here, 0
    )
    came = []
    for step in (1, 2, 3):
        leaving = lax.dynamic_index_in_dim(planes, (here + step) % 4, 1, False)
        came.append(lax.ppermute(leaving, "zh", [(d, (d + step) % 4) for d in range(4)]))
    for step in (1, 2, 3):
        held = lax.dynamic_update_slice_in_dim(held, came[step - 1][None], (here - step) % 4, 0)
    return jnp.transpose(held, (3, 0, 1, 2, 4)).reshape(depth * 64 * own, columns)


def rounded(x):
    return lax.reduce_precision(x, 8, 7).astype(BF16)


def project(control, observe, capacity, conduct):
    col_rows = control.shape[0]
    local_cells = control.shape[1] * control.shape[2] * control.shape[3]
    before, after = neighbours(control)
    coefficients = jnp.stack([capacity, conduct])
    coefficients_before, coefficients_after = neighbours(coefficients)
    relaid = replane(observe)
    capacities, conducts = jnp.concatenate(
        [coefficients_before, coefficients, coefficients_after], axis=1
    )
    control_wide = jnp.concatenate([before, control, after], axis=1)
    widened = rounded(capacities * control_wide.astype(F32))
    applied = (capacity * mass_apply(widened.astype(F32))).astype(BF16)
    applied_flat = applied.reshape(col_rows, local_cells)
    applied_all = relayed(applied_flat, lax.ppermute(applied_flat, "zl", SWAP), 0)
    part = jnp.dot(applied_all, relaid, preferred_element_type=F32)
    relaid, part = lax.optimization_barrier((relaid, part))
    across = lax.ppermute(relaid, "zl", SWAP)
    pieces = lax.all_to_all(part, ("x", "y"), split_axis=0, concat_axis=0, tiled=True)
    pieces, across = lax.optimization_barrier((pieces, across))
    relaid_all = relayed(relaid, across, 1)
    chunk = jnp.sum(pieces.reshape(16, COLS // 16, OWN), axis=0)
    spread_out = jnp.broadcast_to(chunk, (8, COLS // 16, OWN))
    pair = lax.all_to_all(spread_out, ("zh", "zl"), split_axis=0, concat_axis=0, tiled=True)
    pair = jnp.sum(pair.reshape(4, 2, COLS // 16, OWN), axis=0)
    pair = pair.reshape(2, 1, 1, COLS // 16, OWN)
    control_flat = control_wide.reshape(col_rows, 3 * local_cells)
    control_flat, pair = lax.optimization_barrier((control_flat, pair))
    control_all = turned(control_flat)
    left_half = gather_four(pair[..., :LANES], "x", 1)
    right_half = gather_four(pair[..., LANES:], "y", 2)
    left_half = gather_four(left_half, "y", 2).reshape(2, COLS, LANES)
    right_half = gather_four(right_half, "x", 1).reshape(2, COLS, LANES)
    left_other = lax.ppermute(left_half, "core", SWAP)
    right_other = lax.ppermute(right_half, "core", SWAP)
    where = jnp.stack([lax.axis_index(RANK), lax.axis_index("core")]).astype(jnp.int32)
    inverse_low, project_low = factor(where, left_half, right_half, left_other, right_other)
    right_basis = jnp.dot(inverse_low, control_all, preferred_element_type=F32)
    right_basis = right_basis.reshape(control_wide.shape)
    scaled_right = rounded(conducts * right_basis)
    stiff_basis = (-(conduct * stiff_apply(scaled_right.astype(F32)))).astype(BF16)
    left_sum = lax.dot_general(
        project_low, relaid_all, (((1,), (1,)), ((), ())), preferred_element_type=F32
    )
    left_basis = left_sum.astype(BF16).reshape(control.shape)
    return (left_basis, stiff_basis)


def solution(mesh):
    torus = Mesh(mesh.devices.reshape(4, 4, 4, 2, 2), ROWS + RANK)
    in_specs = (
        P(RANK, ROWS, None, None),
        P(RANK, None, ROWS, None),
        P(ROWS, None, None),
        P(ROWS, None, None),
    )
    out_specs = (P(RANK, ROWS, None, None), P(RANK, ROWS, None, None))
    return jax.shard_map(project, mesh=torus, in_specs=in_specs, out_specs=out_specs, check_vma=False)
```

```python
import jax
import jax.numpy as jnp
from jax import lax
from jax.experimental import pallas as pl
from jax.experimental.pallas import tpu as pltpu
from jax.sharding import Mesh
from jax.sharding import PartitionSpec as P


ONE_SIXTH = 1.0 / 6.0
F32 = jnp.float32
BF16 = jnp.bfloat16
ROWS = ("zh", "x", "y")
RANK = ("zl", "core")
COLS = 1024
OWN = 256
SIDE = 128
TILES = COLS // SIDE
LANES = 128
GROUP = 8


def neighbours(x):
    count = lax.axis_size(ROWS)
    up = [(i, i + 1) for i in range(count - 1)]
    down = [(j, i) for i, j in up]
    before = lax.ppermute(x, ROWS, up)
    after = lax.ppermute(x, ROWS, down)
    return before, after


def spread(padded, along_dim, side_weight, centre):
    length = padded.shape[along_dim] - 2
    before = lax.slice_in_dim(padded, 0, length, axis=along_dim)
    middle = lax.slice_in_dim(padded, 1, length + 1, axis=along_dim)
    beyond = lax.slice_in_dim(padded, 2, length + 2, axis=along_dim)
    return side_weight * (before + beyond) + centre * middle


def apply_line(values, along_dim, side_weight, centre):
    widths = [(0, 0)] * values.ndim
    widths[along_dim] = (1, 1)
    return spread(jnp.pad(values, widths), along_dim, side_weight, centre)


def mass_apply(padded):
    result = spread(padded, 1, ONE_SIXTH, 4.0 * ONE_SIXTH)
    result = apply_line(result, 2, ONE_SIXTH, 4.0 * ONE_SIXTH)
    return apply_line(result, 3, ONE_SIXTH, 4.0 * ONE_SIXTH)


def stiff_apply(padded):
    mass_x = spread(padded, 1, ONE_SIXTH, 4.0 * ONE_SIXTH)
    stiff_x = spread(padded, 1, -1.0, 2.0)
    first = apply_line(
        apply_line(stiff_x, 3, ONE_SIXTH, 4.0 * ONE_SIXTH), 2, ONE_SIXTH, 4.0 * ONE_SIXTH
    )
    second = apply_line(apply_line(mass_x, 3, -1.0, 2.0), 2, ONE_SIXTH, 4.0 * ONE_SIXTH)
    third = apply_line(apply_line(mass_x, 3, ONE_SIXTH, 4.0 * ONE_SIXTH), 2, -1.0, 2.0)
    return first + second + third


def halves(x):
    high = x.astype(BF16)
    return high, (x - high.astype(F32)).astype(BF16)


def product(a, b, a_dim=1, b_dim=0):
    dims = (((a_dim,), (b_dim,)), ((), ()))

    def one(p, q):
        return lax.dot_general(p, q, dims, preferred_element_type=F32)

    return one(a[0], b[0]) + (one(a[0], b[1]) + one(a[1], b[0]))


def factor_block(block):
    lane = lax.broadcasted_iota(jnp.int32, (GROUP, SIDE), 1)
    sub = lax.broadcasted_iota(jnp.int32, (GROUP, SIDE), 0)
    count = SIDE // GROUP

    def wide(row):
        return jnp.broadcast_to(row, (GROUP, SIDE))

    def columns(tile, base):
        return [wide(tile[:, base + t : base + t + 1]) for t in range(GROUP)]

    rows = [block[GROUP * v : GROUP * (v + 1), :] for v in range(count)]
    own = columns(rows[0], 0)
    out = []
    for g in range(count):
        base = g * GROUP
        inside = (lane >= base) & (lane < base + GROUP)
        body = jnp.where(inside, 0.0, rows[g])
        pivots = jnp.ones((GROUP, SIDE), F32)
        uppers, inverses, pivot_rows = [], [], []
        for s in range(GROUP):
            pivot = wide(own[s][s : s + 1, :])
            inverse = 1.0 / pivot
            upper = {t: wide(own[t][s : s + 1, :]) for t in range(s + 1, GROUP)}
            taken = jnp.where(sub > s, own[s] * inverse, 0.0)
            pivot_row = jnp.where(lane == base + s, 1.0, wide(body[s : s + 1, :]))
            for t in range(s + 1, GROUP):
                own[t] = own[t] - taken * upper[t]
            body = body - taken * pivot_row
            pivots = jnp.where(sub == s, pivot, pivots)
            uppers.append(upper)
            inverses.append(inverse)
            pivot_rows.append(pivot_row)
        for v in range(g + 1, count):
            cols = columns(rows[v], base)
            new = jnp.where(inside, 0.0, rows[v])
            ahead = columns(rows[v], base + GROUP) if v == g + 1 else []
            for s in range(GROUP):
                taken = cols[s] * inverses[s]
                ahead = [a - taken * wide(cols[s][t : t + 1, :]) for t, a in enumerate(ahead)]
                for t in range(s + 1, GROUP):
                    cols[t] = cols[t] - taken * uppers[s][t]
                new = new - taken * pivot_rows[s]
            rows[v] = new
            own = ahead or own
        low = jnp.where(lane == sub + base, 1.0, jnp.where(lane < base + GROUP, body, 0.0))
        scale = lax.rsqrt(pivots)
        scale = scale * (1.5 - 0.5 * pivots * scale * scale)
        out.append(low * scale)
    return jnp.concatenate(out, axis=0)


def factor_kernel(where, left, right, left_other, right_other, inv_out, proj_out, high, low, m, r_left, r_right):
    core = where[1]
    strip = OWN // 4

    def load(r, squares):
        inner = pl.ds(pl.multiple_of(r * strip, strip), strip)
        for half, pair in enumerate(((left, left_other), (right, right_other))):
            for chip in range(2):
                for other, source in enumerate(pair):
                    block = chip * 2 + (core if other == 0 else 1 - core)
                    lanes = pl.ds(pl.multiple_of(block * OWN + half * LANES, LANES), LANES)
                    x = source[chip, inner, :]
                    for at in range(0, strip, GROUP):
                        squares = squares + x[at : at + GROUP] * x[at : at + GROUP]
                    upper, lower = halves(x)
                    target = (block ^ (r // 4)) * OWN + (r % 4) * strip
                    rows = pl.ds(pl.multiple_of(target, strip), strip)
                    high[rows, lanes] = upper
                    low[rows, lanes] = lower
        return squares

    squares = lax.fori_loop(0, COLS // strip, load, jnp.zeros((GROUP, LANES), F32))
    total = jnp.sum(jnp.sum(squares, axis=0, keepdims=True), axis=1, keepdims=True)
    level = total / COLS + 1e-6
    scale = 1.0 / level
    eye = (lax.broadcasted_iota(jnp.int32, (SIDE, SIDE), 0) == lax.broadcasted_iota(jnp.int32, (SIDE, SIDE), 1)).astype(F32)

    def gram(a, carry):
        left_rows = pl.ds(pl.multiple_of(a * OWN, OWN), OWN)

        def one(b, inner):
            right_rows = pl.ds(pl.multiple_of(b * OWN, OWN), OWN)
            pair = product(
                (high[left_rows, :], low[left_rows, :]),
                (high[right_rows, :], low[right_rows, :]),
                1,
                1,
            )
            m[left_rows, right_rows] = pair * scale
            return inner

        return lax.fori_loop(a, COLS // OWN, one, carry)

    lax.fori_loop(0, COLS // OWN, gram, 0)

    def step(k, carry):
        block = pl.ds(pl.multiple_of(k * SIDE, SIDE), SIDE)
        x = factor_block(m[block, block] + eye)
        m[block, block] = eye
        r = product(halves(x), halves(m[block, :]))
        m[block, :] = r
        upper, lower = halves(r)
        for at, (one, two) in enumerate(((upper, upper), (upper, lower), (lower, upper))):
            r_left[at * SIDE : (at + 1) * SIDE, :] = one
            r_right[at * SIDE : (at + 1) * SIDE, :] = two

        def update(i, inner):
            rows = pl.ds(pl.multiple_of(i * SIDE, SIDE), SIDE)
            m[rows, block] = jnp.zeros((SIDE, SIDE), F32)
            taken = lax.dot_general(
                r_left[:, rows], r_right[...], (((0,), (0,)), ((), ())), preferred_element_type=F32
            )
            m[rows, :] = m[rows, :] - taken
            return inner

        lax.fori_loop(k + 1, TILES, update, 0)
        return carry

    lax.fori_loop(0, TILES, step, 0)
    first = pl.multiple_of(where[0] * OWN, OWN)
    row = lax.broadcasted_iota(jnp.int32, (OWN, OWN), 0)
    column = lax.broadcasted_iota(jnp.int32, (OWN, OWN), 1)
    own = []
    for block in range(4):
        part = m[pl.ds(first, OWN), block * OWN : (block + 1) * OWN]
        own.append(jnp.where(column + block * OWN <= row + first, part, 0.0))
    own = halves(jnp.concatenate(own, axis=1))
    shrink = lax.rsqrt(level)

    def project(turn, carry):
        block = where[0] ^ turn
        lanes = pl.ds(pl.multiple_of(block * OWN, OWN), OWN)
        out = pl.ds(pl.multiple_of(turn * OWN, OWN), OWN)
        part = m[pl.ds(first, OWN), lanes]
        part = jnp.where(column + block * OWN <= row + first, part, 0.0)
        inv_out[:, out] = part.astype(BF16)
        proj_out[:, out] = (product(own, (high[:, lanes], low[:, lanes])) * shrink).astype(BF16)
        return carry

    lax.fori_loop(0, 4, project, 0)


def factor(where, left, right, left_other, right_other):
    vmem = pl.BlockSpec(memory_space=pltpu.VMEM)
    return pl.pallas_call(
        factor_kernel,
        out_shape=(jax.ShapeDtypeStruct((OWN, COLS), BF16),) * 2,
        in_specs=[pl.BlockSpec(memory_space=pltpu.SMEM)] + [vmem] * 4,
        out_specs=[vmem] * 2,
        scratch_shapes=[
            pltpu.VMEM((COLS, COLS), BF16),
            pltpu.VMEM((COLS, COLS), BF16),
            pltpu.VMEM((COLS, COLS), F32),
            pltpu.VMEM((3 * SIDE, COLS), BF16),
            pltpu.VMEM((3 * SIDE, COLS), BF16),
        ],
        compiler_params=pltpu.CompilerParams(vmem_limit_bytes=20 * 2**20),
    )(where, left, right, left_other, right_other)


def gather_four(x, axis, dim):
    here = lax.axis_index(axis)
    shape = list(x.shape)
    shape[dim] = 4
    full = lax.dynamic_update_slice_in_dim(jnp.zeros(shape, x.dtype), x, here, dim)
    for step in (1, 2, 3):
        moved = lax.ppermute(x, axis, [(d, (d + step) % 4) for d in range(4)])
        full = lax.dynamic_update_slice_in_dim(full, moved, (here - step) % 4, dim)
    return full


def turned(x):
    moved = [lax.ppermute(x, RANK, [(d, d ^ step) for d in range(4)]) for step in (1, 2, 3)]
    return jnp.concatenate([x] + moved, axis=0)


SWAP = [(0, 1), (1, 0)]


def relayed(x, across, axis):
    near = lax.ppermute(x, "core", SWAP)
    return jnp.concatenate([x, near, across, lax.ppermute(across, "core", SWAP)], axis=axis)


def replane(observe):
    columns, depth, own, _ = observe.shape
    planes = jnp.transpose(observe.reshape(columns, depth, own, 4, 16), (4, 3, 2, 1, 0))
    planes = lax.all_to_all(planes, ("x", "y"), split_axis=0, concat_axis=0, tiled=True)
    here = lax.axis_index("zh")
    held = jnp.zeros((4, 16, own, depth, columns), observe.dtype)
    held = lax.dynamic_update_slice_in_dim(
        held, lax.dynamic_index_in_dim(planes, here, 1, False)[None], here, 0
    )
    came = []
    for step in (1, 2, 3):
        leaving = lax.dynamic_index_in_dim(planes, (here + step) % 4, 1, False)
        came.append(lax.ppermute(leaving, "zh", [(d, (d + step) % 4) for d in range(4)]))
    for step in (1, 2, 3):
        held = lax.dynamic_update_slice_in_dim(held, came[step - 1][None], (here - step) % 4, 0)
    return jnp.transpose(held, (3, 0, 1, 2, 4)).reshape(depth * 64 * own, columns)


def rounded(x):
    return lax.reduce_precision(x, 8, 7).astype(BF16)


def project(control, observe, capacity, conduct):
    col_rows = control.shape[0]
    local_cells = control.shape[1] * control.shape[2] * control.shape[3]
    before, after = neighbours(control)
    coefficients = jnp.stack([capacity, conduct])
    coefficients_before, coefficients_after = neighbours(coefficients)
    relaid = replane(observe)
    capacities, conducts = jnp.concatenate(
        [coefficients_before, coefficients, coefficients_after], axis=1
    )
    control_wide = jnp.concatenate([before, control, after], axis=1)
    widened = rounded(capacities * control_wide.astype(F32))
    applied = (capacity * mass_apply(widened.astype(F32))).astype(BF16)
    applied_flat = applied.reshape(col_rows, local_cells)
    applied_all = relayed(applied_flat, lax.ppermute(applied_flat, "zl", SWAP), 0)
    part = jnp.dot(applied_all, relaid, preferred_element_type=F32)
    relaid, part = lax.optimization_barrier((relaid, part))
    across = lax.ppermute(relaid, "zl", SWAP)
    pieces = lax.all_to_all(part, ("x", "y"), split_axis=0, concat_axis=0, tiled=True)
    pieces, across = lax.optimization_barrier((pieces, across))
    relaid_all = relayed(relaid, across, 1)
    chunk = jnp.sum(pieces.reshape(16, COLS // 16, OWN), axis=0)
    spread_out = jnp.broadcast_to(chunk, (8, COLS // 16, OWN))
    pair = lax.all_to_all(spread_out, ("zh", "zl"), split_axis=0, concat_axis=0, tiled=True)
    pair = jnp.sum(pair.reshape(4, 2, COLS // 16, OWN), axis=0)
    pair = pair.reshape(2, 1, 1, COLS // 16, OWN)
    control_flat = control_wide.reshape(col_rows, 3 * local_cells)
    control_flat, pair = lax.optimization_barrier((control_flat, pair))
    control_all = turned(control_flat)
    left_half = gather_four(pair[..., :LANES], "x", 1)
    right_half = gather_four(pair[..., LANES:], "y", 2)
    left_half = gather_four(left_half, "y", 2).reshape(2, COLS, LANES)
    right_half = gather_four(right_half, "x", 1).reshape(2, COLS, LANES)
    left_other = lax.ppermute(left_half, "core", SWAP)
    right_other = lax.ppermute(right_half, "core", SWAP)
    where = jnp.stack([lax.axis_index(RANK), lax.axis_index("core")]).astype(jnp.int32)
    inverse_low, project_low = factor(where, left_half, right_half, left_other, right_other)
    right_basis = jnp.dot(inverse_low, control_all, preferred_element_type=F32)
    right_basis = right_basis.reshape(control_wide.shape)
    scaled_right = rounded(conducts * right_basis)
    stiff_basis = (-(conduct * stiff_apply(scaled_right.astype(F32)))).astype(BF16)
    left_sum = lax.dot_general(
        project_low, relaid_all, (((1,), (1,)), ((), ())), preferred_element_type=F32
    )
    left_basis = left_sum.astype(BF16).reshape(control.shape)
    return (left_basis, stiff_basis)


def solution(mesh):
    torus = Mesh(mesh.devices.reshape(4, 4, 4, 2, 2), ROWS + RANK)
    in_specs = (
        P(RANK, ROWS, None, None),
        P(RANK, None, ROWS, None),
        P(ROWS, None, None),
        P(ROWS, None, None),
    )
    out_specs = (P(RANK, ROWS, None, None), P(RANK, ROWS, None, None))
    return jax.shard_map(project, mesh=torus, in_specs=in_specs, out_specs=out_specs, check_vma=False)
```
